32 devices in a mesh: grp: 2 (over y), tile: 4 (over z), tm: 2 (over x), ch: 2 (over core).
Axes of the slice: x: 2, y: 2, z: 4, core: 2. Of those that a mesh axis runs over, the one named last changes fastest.
Arguments:
- latent: bfloat16 [8, 8, 64, 512], P(('grp', 'tm'), None, 'tile', 'ch'), parts along dimension 0, may hold values from -340 to 340
- norm_gain: float32 [512], P('ch'), may hold values from 0.1 to 1.9
- norm_shift: float32 [512], P('ch'), may hold values from -3 to 3
- kernel: bfloat16 [3, 3, 3, 512, 512], P(None, None, None, ('ch', 'tile', 'tm')), may hold values from -0.0546875 to 0.0546875
- conv_bias: float32 [512], P('ch'), may hold values from -3 to 3
- blend_profile: int32 [4], replicated, may hold values from 0 to 3
Outputs:
- decoded: bfloat16 [8, 8, 64, 512], P(('grp', 'tm'), None, 'tile', 'ch'), parts along dimension 0
The draws below stay inside these ranges and needn't reach their ends.
There are 2 independent parts, one for each index of `grp`. The reference program is written for one: setup_inputs(seed, part) draws one part's arguments, and reference() takes and returns one part's arrays. A program takes and returns all parts, laid end to end along the dimension named above; an argument that names none is the same for every part. Nothing has to cross between parts.
All inputs are finite; a program needn't handle non-finite values.
Results may differ from the reference program's by a relative error of at most 0.0038.
The reference program's roundings to bfloat16 on the way count: a program that leaves them out, or rounds other values in their place, can miss the bound.
Values may be sent and summed in bfloat16 or wider, within the bound.
A program may use at most 64 MiB of HBM per device.

```python
import math
import jax
import jax.numpy as jnp
from jax import lax

CHANNELS = 512
GROUPS = 32
ROWS = 8
TW = 16
RIM = 4
FRAMES = 4
TILES = 4
WIDTH = 64


def draw_latent(key, part):
    key_base, key_cell, key_chan = jax.random.split(key, 3)
    full_shape = (FRAMES, ROWS, WIDTH, CHANNELS)
    chan_scale = jnp.exp(jax.random.uniform(key_chan, (1, 1, 1, CHANNELS), jnp.float32, -1.2, 1.2))
    cell_scale = jnp.exp(jax.random.uniform(key_cell, (FRAMES, ROWS, WIDTH, 1), jnp.float32) * math.log(10.0))
    base = jnp.clip(jax.random.normal(key_base, full_shape, jnp.float32), -4.0, 4.0)
    return (base * cell_scale * chan_scale).astype(jnp.bfloat16)


def place_ends(array, rng, smallest, high):
    longest = array.shape.index(max(array.shape))
    spots = []
    for shift in (0, 1):
        where = [jax.random.randint(jax.random.fold_in(rng, axis), (), 0, length) for axis, length in enumerate(array.shape)]
        where[longest] = (where[longest] + shift) % array.shape[longest]
        spots.append(tuple(where))
    return array.at[spots[0]].set(smallest).at[spots[1]].set(high)


def levels(key, shape, shards, smallest, largest):
    level, own = 1.0, jax.random.fold_in(key, 6)
    for dim, shards_of in shards:
        steps = jnp.exp(jax.random.uniform(jax.random.fold_in(own, dim), (shards_of,), jnp.float32, smallest / len(shards), largest / len(shards)))
        level = level * jnp.repeat(steps, shape[dim] // shards_of).reshape([-1 if axis == dim else 1 for axis in range(len(shape))])
    return level


def bell_draw(stream_key, extent, scale, reach, pieces=(), kind=jnp.bfloat16):
    result = jax.random.normal(stream_key, extent, jnp.float32) * scale
    if len(pieces) > 0:
        result = levels(stream_key, extent, pieces, -0.22, 0.18) * result
    return jnp.clip(result, min=-reach, max=reach).astype(kind)


def setup_inputs(seed: int = 0, part: int = 0) -> dict:
    splits = jax.random.split(jax.random.key(seed), 7)
    part_splits = jax.random.split(jax.random.fold_in(splits[6], part), 7)
    latent = draw_latent(jax.random.fold_in(jax.random.fold_in(splits[6], part), 71), part)
    norm_gain = jnp.clip(1.0 + 0.18 * jax.random.normal(splits[1], (CHANNELS,), jnp.float32), 0.1, 1.9)
    norm_shift = bell_draw(splits[2], (CHANNELS,), 0.5, 3.0, ((0, 2),), jnp.float32)
    kernel = bell_draw(splits[3], (3, 3, 3, CHANNELS, CHANNELS), (27 * CHANNELS) ** -0.5, 0.0546875, ((3, 16),))
    conv_bias = bell_draw(splits[4], (CHANNELS,), 0.3, 3.0, ((0, 2),), jnp.float32)
    blend_profile = place_ends(jax.random.randint(splits[5], (TILES,), 0, 4), jax.random.fold_in(splits[5], 1), 0, 3).astype(jnp.int32)
    return {"latent": latent, "norm_gain": norm_gain, "norm_shift": norm_shift, "kernel": kernel, "conv_bias": conv_bias, "blend_profile": blend_profile}


def ramp_weight(profile, position, margin):
    fraction = (position.astype(jnp.float32) + 0.5) / (2.0 * margin)
    exponent = 1.0 + profile.astype(jnp.float32)
    near_part = jnp.power(1.0 - fraction, exponent)
    far_part = jnp.power(fraction, exponent)
    return near_part / (near_part + far_part)

def frame_stats(values, colmask, groups):
    frame_count, row_count, col_count, chan_count = values.shape
    grouped = values.reshape(frame_count, row_count, col_count, groups, chan_count // groups)
    weight = colmask.reshape(1, 1, col_count, 1, 1)
    counted = row_count * (chan_count // groups) * jnp.sum(colmask)
    center = lax.optimization_barrier(jnp.sum(grouped * weight, axis=(1, 2, 4))) / counted
    spread = (grouped - center[:, None, None, :, None]) * weight
    inverse = lax.rsqrt(lax.optimization_barrier(jnp.sum(spread * spread, axis=(1, 2, 4))) / counted + 1e-06)
    return (center, inverse)

def activate(values, center, inverse, norm_gain, norm_shift, colmask, timemask, groups):
    frame_count, row_count, col_count, chan_count = values.shape
    grouped = values.reshape(frame_count, row_count, col_count, groups, chan_count // groups)
    normed = (grouped - center[:, None, None, :, None]) * inverse[:, None, None, :, None]
    normed = normed.reshape(values.shape) * norm_gain + norm_shift
    masked = jax.nn.silu(normed) * colmask[None, None, :, None] * timemask[:, None, None, None]
    return masked.astype(jnp.bfloat16)

def conv_taps(padded, kernel_part, frame_count, row_count, col_count):
    in_width = kernel_part.shape[3]
    running = None
    for tap_time in range(3):
        for tap_row in range(3):
            for tap_col in range(3):
                window = padded[tap_time:tap_time + frame_count, tap_row:tap_row + row_count, tap_col:tap_col + col_count]
                contrib = jnp.dot(window.reshape(-1, in_width), kernel_part[tap_time, tap_row, tap_col], preferred_element_type=jnp.float32)
                running = contrib if running is None else running + contrib
    return running

def reference(latent, norm_gain, norm_shift, kernel, conv_bias, blend_profile):
    cols_all = TW + 2 * RIM

    def one_tile(tile_pos):
        column = tile_pos * TW - RIM + jnp.arange(cols_all, dtype=jnp.int32)
        colmask = ((column >= 0) & (column < WIDTH)).astype(jnp.float32)
        picked = jnp.take(latent, jnp.clip(column, 0, WIDTH - 1).astype(jnp.int32), axis=2).astype(jnp.float32)
        picked = picked * colmask[None, None, :, None]
        center, inverse = frame_stats(picked, colmask, GROUPS)
        timemask = jnp.ones((FRAMES,), jnp.float32)
        activated = activate(picked, center, inverse, norm_gain, norm_shift, colmask, timemask, GROUPS)
        padded = jnp.pad(activated, ((2, 0), (1, 1), (1, 1), (0, 0)))
        running = conv_taps(padded, kernel, FRAMES, ROWS, cols_all)
        return (running.reshape(FRAMES, ROWS, cols_all, CHANNELS) + conv_bias).astype(jnp.bfloat16)
    outputs = lax.map(one_tile, jnp.arange(TILES, dtype=jnp.int32))
    own_all = outputs[:, :, :, RIM:RIM + TW].astype(jnp.float32)
    zero_tile = jnp.zeros_like(outputs[:1])
    before = jnp.concatenate([zero_tile, outputs[:-1]], axis=0)
    after = jnp.concatenate([outputs[1:], zero_tile], axis=0)
    left_nbr = before[:, :, :, TW + RIM:].astype(jnp.float32)
    right_nbr = after[:, :, :, :RIM].astype(jnp.float32)
    tile_ids = jnp.arange(TILES, dtype=jnp.int32)
    offsets = jnp.arange(RIM, dtype=jnp.int32)
    prev_profile = jnp.concatenate([blend_profile[:1], blend_profile[:-1]])
    left_weight = jnp.where(tile_ids[:, None] > 0, ramp_weight(prev_profile[:, None], offsets[None, :] + RIM, RIM), 0.0)
    right_weight = jnp.where(tile_ids[:, None] < TILES - 1, ramp_weight(blend_profile[:, None], offsets[None, :], RIM), 1.0)
    left_wide = left_weight[:, None, None, :, None]
    right_wide = right_weight[:, None, None, :, None]
    head_cols = own_all[:, :, :, :RIM] * (1.0 - left_wide) + left_nbr * left_wide
    tail_cols = own_all[:, :, :, TW - RIM:] * right_wide + right_nbr * (1.0 - right_wide)
    middle = own_all[:, :, :, RIM:TW - RIM]
    core_all = jnp.concatenate([head_cols, middle, tail_cols], axis=3)
    return jnp.moveaxis(core_all, 0, 2).reshape(FRAMES, ROWS, WIDTH, CHANNELS).astype(jnp.bfloat16)
```

```python
import functools
import jax
import jax.numpy as jnp
from jax import lax
from jax.experimental import pallas as pl
from jax.experimental.pallas import tpu as pltpu
from jax.sharding import PartitionSpec as P

GROUPS = 32
RIM = 4


def with_halo(shard, sides, width):
    for axis, dim in sides:
        size, length = (lax.axis_size(axis), shard.shape[dim])
        up = [(i, (i + 1) % size) for i in range(size - 1)]
        down = [(j, i) for i, j in up]
        last = lax.slice_in_dim(shard, length - width, length, axis=dim)
        leading = lax.slice_in_dim(shard, 0, width, axis=dim)
        before = lax.ppermute(last, axis, up)
        after = lax.ppermute(leading, axis, down)
        shard = jnp.concatenate([before, shard, after], axis=dim)
    return shard


def passed_along(block, axis, distance):
    devices = range(lax.axis_size(axis))
    route = [(i - distance, i) for i in devices if i - distance in devices]
    return lax.ppermute(block, axis, route)


def ramp_weight(profile, position, margin):
    fraction = (position.astype(jnp.float32) + 0.5) / (2.0 * margin)
    exponent = 1.0 + profile.astype(jnp.float32)
    near_part = jnp.power(1.0 - fraction, exponent)
    far_part = jnp.power(fraction, exponent)
    return near_part / (near_part + far_part)


def frame_stats(values, colmask, groups):
    frame_count, row_count, col_count, chan_count = values.shape
    grouped = values.reshape(frame_count, row_count, col_count, groups, chan_count // groups)
    weight = colmask.reshape(1, 1, col_count, 1, 1)
    counted = row_count * (chan_count // groups) * jnp.sum(colmask)
    center = jnp.sum(grouped * weight, axis=(1, 2, 4)) / counted
    spread = (grouped - center[:, None, None, :, None]) * weight
    inverse = lax.rsqrt(jnp.sum(spread * spread, axis=(1, 2, 4)) / counted + 1e-06)
    return (center, inverse)


def activate(values, center, inverse, norm_gain, norm_shift, colmask, timemask, groups):
    frame_count, row_count, col_count, chan_count = values.shape
    grouped = values.reshape(frame_count, row_count, col_count, groups, chan_count // groups)
    normed = (grouped - center[:, None, None, :, None]) * inverse[:, None, None, :, None]
    normed = normed.reshape(values.shape) * norm_gain + norm_shift
    masked = jax.nn.silu(normed) * colmask[None, None, :, None] * timemask[:, None, None, None]
    return masked.astype(jnp.bfloat16)


def conv_taps(padded, kernel_part, frame_count, row_count, col_count):
    in_width = kernel_part.shape[3]
    running = None
    for tap_time in range(3):
        for tap_row in range(3):
            for tap_col in range(3):
                window = padded[
                    tap_time : tap_time + frame_count,
                    tap_row : tap_row + row_count,
                    tap_col : tap_col + col_count,
                ]
                contrib = jnp.dot(
                    window.reshape(-1, in_width),
                    kernel_part[tap_time, tap_row, tap_col],
                    preferred_element_type=jnp.float32,
                )
                running = contrib if running is None else running + contrib
    return running


def gathered_on_device(latent, norm_gain, norm_shift, kernel, conv_bias, blend_profile):
    frame_count, row_count, core_cols, chan_half = latent.shape
    out_chans = kernel.shape[4]
    groups = GROUPS // lax.axis_size("ch")
    ncols = core_cols + 2 * RIM
    tile_pos = lax.axis_index("tile")
    tile_count = lax.axis_size("tile")
    window_in = with_halo(latent, (("tile", 2),), RIM)
    cached = passed_along(window_in, "tm", 1)
    frames = jnp.concatenate([cached, window_in], axis=0).astype(jnp.float32)
    column = tile_pos * core_cols - RIM + jnp.arange(ncols, dtype=jnp.int32)
    colmask = ((column >= 0) & (column < tile_count * core_cols)).astype(jnp.float32)
    started = (lax.axis_index("tm") > 0).astype(jnp.float32)
    timemask = jnp.concatenate(
        [jnp.ones((2,), jnp.float32) * started, jnp.ones((frame_count,), jnp.float32)]
    )
    center, inverse = frame_stats(frames, colmask, groups)
    activated = activate(frames, center, inverse, norm_gain, norm_shift, colmask, timemask, groups)
    inputs = (jnp.pad(activated, ((0, 0), (1, 1), (1, 1), (0, 0))),)
    widths = (ncols,)

    def accumulate(shard_rows):
        return tuple(
            (
                conv_taps(source, shard_rows, frame_count, row_count, width_cols)
                for source, width_cols in zip(inputs, widths)
            )
        )

    totals = accumulate(lax.all_gather(kernel, ("tile", "tm"), axis=3, tiled=True))
    shaped = [
        running.reshape(frame_count, row_count, width_cols, out_chans)
        for running, width_cols in zip(totals, widths)
    ]
    joined = shaped[0]
    summed = lax.psum_scatter(joined, "ch", scatter_dimension=3, tiled=True)
    tile_out = (summed + conv_bias).astype(jnp.bfloat16)
    extended = with_halo(tile_out, (("tile", 2),), RIM)
    own_out = tile_out[:, :, RIM : RIM + core_cols]
    left_nbr = extended[:, :, :RIM]
    right_nbr = extended[:, :, ncols + RIM :]
    own_profile = lax.dynamic_index_in_dim(blend_profile, tile_pos, 0, keepdims=False)
    prev_profile = lax.dynamic_index_in_dim(
        blend_profile, jnp.maximum(tile_pos - 1, 0), 0, keepdims=False
    )
    offsets = jnp.arange(RIM, dtype=jnp.int32)
    left_weight = jnp.where(tile_pos > 0, ramp_weight(prev_profile, offsets + RIM, RIM), 0.0)
    right_weight = jnp.where(tile_pos < tile_count - 1, ramp_weight(own_profile, offsets, RIM), 1.0)
    left_wide = left_weight[None, None, :, None]
    right_wide = right_weight[None, None, :, None]
    own_float = own_out.astype(jnp.float32)
    head_cols = own_float[:, :, :RIM] * (1.0 - left_wide) + left_nbr.astype(jnp.float32) * left_wide
    tail_cols = own_float[:, :, core_cols - RIM :] * right_wide + right_nbr.astype(jnp.float32) * (
        1.0 - right_wide
    )
    middle = own_float[:, :, RIM : core_cols - RIM]
    return jnp.concatenate([head_cols, middle, tail_cols], axis=2).astype(jnp.bfloat16)


MESH = pl.DeviceIdType.MESH
TILES = 4
BLOCKS = 2
PARTS = TILES * BLOCKS
ROWS = 8
TW = 16
WIN = TW + 2 * RIM
IN = 32
FRAMES = 4
HALF = 256
OUT = 512
F32 = jnp.float32
BF16 = jnp.bfloat16


def iota(shape, dim):
    return lax.broadcasted_iota(jnp.int32, shape, dim)


def exact_dot(a, b):
    return jnp.dot(a, b, preferred_element_type=F32, precision=lax.Precision.HIGHEST)


def fused_kernel(
    profile, latent, gain, shift, kernel, bias, out,
    weights, packed, arrived, grid, act, sums, centers, inverses, ramp, lhs, conv,
    keep, give, took, cross, crossed, send, landed,
    w_sem, a_send, a_recv, s_send, s_recv, x_send, x_recv, z_send, z_recv,
):
    tile = lax.axis_index("tile")
    tm = lax.axis_index("tm")
    ch = lax.axis_index("ch")
    me = tile * BLOCKS + tm

    loads = []
    for a in range(3):
        for e in range(3):
            for side in range(2):
                start = pl.multiple_of(((ch + side) % 2) * HALF, HALF)
                loads.append(
                    pltpu.make_async_copy(
                        kernel.at[a, :, e, :, pl.ds(start, HALF)],
                        weights.at[a * 3 + e, pl.ds(0, 3), :, pl.ds(side * HALF, HALF)],
                        w_sem.at[(a * 3 + e) * 2 + side],
                    )
                )
    for load in loads:
        load.start()

    barrier = pltpu.get_barrier_semaphore()
    for d in range(1, PARTS):
        j = (me + d) % PARTS
        pl.semaphore_signal(
            barrier, inc=1, device_id={"tile": j // BLOCKS, "tm": j % BLOCKS}, device_id_type=MESH
        )
    pl.semaphore_signal(barrier, inc=1, device_id={"ch": 1 - ch}, device_id_type=MESH)

    row_i, col_i = iota((128, 128), 0), iota((128, 128), 1)
    turn = jnp.where((row_i % ROWS) * TW + row_i // ROWS == col_i, 1.0, 0.0).astype(BF16)
    lane_block = iota((64, 128), 1) // IN
    turned = [
        jnp.dot(turn, latent[f].reshape(ROWS * TW, HALF), preferred_element_type=F32)
        for f in range(2)
    ]
    for j in range(PARTS):
        lanes = slice((j // 4) * 128, (j // 4) * 128 + 128)
        joined = None
        for k in range(4):
            piece = turned[k // 2][(k % 2) * 64 : (k % 2) * 64 + 64, lanes]
            amount = ((k - j % 4) * IN) % 128
            if amount:
                piece = pltpu.roll(piece, amount, 1)
            joined = piece if joined is None else jnp.where(lane_block == k, piece, joined)
        packed[j] = joined.astype(BF16)

    pl.semaphore_wait(barrier, PARTS)
    moves = []
    for d in range(1, PARTS):
        j = (me + d) % PARTS
        moves.append(
            pltpu.make_async_remote_copy(
                src_ref=packed.at[j],
                dst_ref=arrived.at[me],
                send_sem=a_send.at[d - 1],
                recv_sem=a_recv.at[d - 1],
                device_id={"tile": j // BLOCKS, "tm": j % BLOCKS},
                device_id_type=MESH,
            )
        )
    for move in moves:
        move.start()
    arrived[me] = packed[me]

    act[:, 0:2] = jnp.zeros((TILES, 2, WIN + 2, ROWS, 128), F32)
    act[:, 2:, 0:1] = jnp.zeros((TILES, FRAMES, 1, ROWS, 128), F32)
    act[:, 2:, WIN + 1 :] = jnp.zeros((TILES, FRAMES, 1, ROWS, 128), F32)
    grid[:, 0:RIM] = jnp.zeros((FRAMES, RIM, ROWS, 128), F32)
    grid[:, RIM + TILES * TW :] = jnp.zeros((FRAMES, RIM, ROWS, 128), F32)
    weights[:, 3] = jnp.zeros((9, IN, OUT), BF16)
    fraction = (iota((8, OUT), 0).astype(F32) + 0.5) / (2.0 * RIM)
    for margin in range(TILES):
        p = jnp.full((8, OUT), profile[margin], jnp.int32)
        near, far = 1.0 - fraction, fraction
        near_part, far_part = near, far
        for power in range(1, 4):
            near_part = jnp.where(p >= power, near_part * near, near_part)
            far_part = jnp.where(p >= power, far_part * far, far_part)
        ramp[margin] = near_part / (near_part + far_part)
    pick = jnp.where(iota((HALF, 128), 0) == me * IN + iota((HALF, 128), 1) % IN, 1.0, 0.0)
    own_gain = exact_dot(jnp.broadcast_to(gain[...], (8, HALF)), pick)
    own_shift = exact_dot(jnp.broadcast_to(shift[...], (8, HALF)), pick)
    group = jnp.where(
        (row_i // (IN // 2)) == (col_i // (IN // 2)), 1.0, 0.0
    )
    spread = [
        jnp.where((row_i // IN == k) & (row_i % IN == col_i % IN), 1.0, 0.0).astype(BF16)
        for k in range(4)
    ]

    for move in moves:
        move.wait()
    everything = arrived[...].reshape(PARTS * 64, 128)
    for k in range(4):
        wide = jnp.dot(everything, spread[k], preferred_element_type=F32)
        for s in range(PARTS):
            first = RIM + (s // BLOCKS) * TW + (k % 2) * (TW // 2)
            grid[(s % BLOCKS) * 2 + k // 2, first : first + TW // 2] = wide[
                s * 64 : s * 64 + 64
            ].reshape(TW // 2, ROWS, 128)

    def present(t):
        column = t * TW + iota((WIN, ROWS, 128), 0)
        return jnp.where((column >= RIM) & (column < RIM + TILES * TW), 1.0, 0.0)

    def totals(n, _):
        t, f = n // FRAMES, n % FRAMES
        sums[n] = jnp.sum(grid[f, pl.ds(t * TW, WIN)], axis=0)
        return 0

    pairs = TILES * FRAMES
    tile_of = iota((pairs, 1, 128), 0) // FRAMES
    counted = jnp.where((tile_of == 0) | (tile_of == TILES - 1), WIN - RIM, WIN).astype(F32)
    counted = counted * float(ROWS * (IN // 2))
    lax.fori_loop(0, pairs, totals, 0)

    def grouped():
        per_group = exact_dot(sums[...].reshape(pairs * ROWS, 128), group)
        return jnp.sum(per_group.reshape(pairs, ROWS, 128), axis=1, keepdims=True) / counted

    centers[...] = jnp.broadcast_to(grouped(), (pairs, ROWS, 128))

    def squares(n, _):
        t, f = n // FRAMES, n % FRAMES
        apart = (grid[f, pl.ds(t * TW, WIN)] - centers[n]) * present(t)
        sums[n] = jnp.sum(apart * apart, axis=0)
        return 0

    lax.fori_loop(0, pairs, squares, 0)
    inverses[...] = jnp.broadcast_to(lax.rsqrt(grouped() + 1e-06), (pairs, ROWS, 128))

    block_of, row_of = iota((ROWS, 128), 1) // IN, iota((ROWS, 128), 0)
    inside = (block_of == 1) | ((block_of == 0) & (row_of > 0))
    inside = jnp.where(inside | ((block_of == 2) & (row_of < ROWS - 1)), 1.0, 0.0)

    def activate_window(n, _):
        t, f = n // FRAMES, n % FRAMES
        v = (grid[f, pl.ds(t * TW, WIN)] - centers[n]) * inverses[n] * own_gain + own_shift
        v = v / (1.0 + jnp.exp(-v)) * present(t)
        before, after = pltpu.roll(v, 1, 1), pltpu.roll(v, ROWS - 1, 1)
        v = jnp.where(block_of == 0, before, jnp.where(block_of == 2, after, v))
        act[t, f + 2, 1 : WIN + 1] = v * inside
        return 0

    lax.fori_loop(0, pairs, activate_window, 0)
    for load in loads:
        load.wait()

    rows_kept = FRAMES * TW * ROWS
    block_rows = rows_kept // BLOCKS

    def sibling_copy(i):
        return pltpu.make_async_remote_copy(
            src_ref=give.at[i], dst_ref=took.at[i],
            send_sem=s_send.at[i], recv_sem=s_recv.at[i],
            device_id={"ch": 1 - ch}, device_id_type=MESH,
        )

    def cross_copy(i):
        return pltpu.make_async_remote_copy(
            src_ref=cross.at[i], dst_ref=crossed.at[i],
            send_sem=x_send.at[i], recv_sem=x_recv.at[i],
            device_id={"tm": 1 - tm}, device_id_type=MESH,
        )

    def owner_copy(i):
        return pltpu.make_async_remote_copy(
            src_ref=send.at[i], dst_ref=landed.at[i],
            send_sem=z_send.at[i], recv_sem=z_recv.at[i],
            device_id={"tile": (tile + 1 + i) % TILES}, device_id_type=MESH,
        )

    own_rows = pl.ds(pl.multiple_of(tm * block_rows, block_rows), block_rows)
    other_rows = pl.ds(pl.multiple_of((1 - tm) * block_rows, block_rows), block_rows)

    def convolve(i):
        t = (tile + 1 + i) % TILES
        left, right = (t + TILES - 1) % TILES, (t + 1) % TILES
        for f in range(FRAMES):
            for a in range(3):
                for e in range(3):
                    lanes = slice((a * 3 + e) * 128, (a * 3 + e) * 128 + 128)
                    row = f * WIN * ROWS
                    for owner, first, count in (
                        (t, RIM, TW), (left, TW + RIM, RIM), (right, 0, RIM),
                    ):
                        piece = act[owner, f + a, first + e : first + e + count]
                        lhs[row : row + count * ROWS, lanes] = piece.reshape(
                            count * ROWS, 128
                        ).astype(BF16)
                        row += count * ROWS
        conv[...] = jnp.dot(
            lhs[...], weights[...].reshape(9 * 128, OUT), preferred_element_type=F32
        )
        has_left = jnp.where(t > 0, 1.0, 0.0)
        has_right = jnp.where(t < TILES - 1, 1.0, 0.0)
        for f in range(FRAMES):
            base = f * WIN * ROWS
            for c in range(TW):
                value = conv[base + c * ROWS : base + (c + 1) * ROWS]
                if c < RIM:
                    w = ramp[left, RIM + c : RIM + c + 1] * has_left
                    far = base + (TW + c) * ROWS
                    value = value * (1.0 - w) + conv[far : far + ROWS] * w
                if c >= TW - RIM:
                    j = c - (TW - RIM)
                    w = 1.0 - (1.0 - ramp[t, j : j + 1]) * has_right
                    far = base + (TW + RIM + j) * ROWS
                    value = value * w + conv[far : far + ROWS] * (1.0 - w)
                row = (f * TW + c) * ROWS
                keep[i, row : row + ROWS] = value[:, :HALF]
                give[i, row : row + ROWS] = value[:, HALF:]
        sibling_copy(i).start()

    def join_sibling(i):
        sibling_copy(i).wait_recv()
        cross[i] = (keep[i, other_rows] + took[i, other_rows]).astype(BF16)
        cross_copy(i).start()

    def join_cross(i):
        cross_copy(i).wait_recv()
        return keep[i, own_rows] + took[i, own_rows] + crossed[i].astype(F32)

    def pass_on(i):
        send[i] = join_cross(i).astype(BF16)
        owner_copy(i).start()

    def step(s, _):
        pl.when(s < TILES)(lambda: convolve(s))
        pl.when((s >= 1) & (s <= TILES))(lambda: join_sibling(s - 1))
        pl.when((s >= 2) & (s <= TILES))(lambda: pass_on(s - 2))
        return 0

    lax.fori_loop(0, TILES + 1, step, 0)
    total = join_cross(TILES - 1)
    for i in range(TILES - 1):
        owner_copy(i).wait_recv()
        total = total + landed[i].astype(F32)
    result = (total + bias[...]).astype(BF16)
    back = jnp.where((row_i % TW) * ROWS + row_i // TW == col_i, 1.0, 0.0).astype(BF16)
    for f in range(2):
        frame = result[f * TW * ROWS : (f + 1) * TW * ROWS]
        out[f] = (
            jnp.dot(back, frame, preferred_element_type=F32)
            .astype(BF16)
            .reshape(ROWS, TW, HALF)
        )
    for i in range(TILES):
        sibling_copy(i).wait_send()
        cross_copy(i).wait_send()
        if i < TILES - 1:
            owner_copy(i).wait_send()


def fused_on_device(latent, norm_gain, norm_shift, kernel, conv_bias, blend_profile):
    block_rows = 2 * TW * ROWS
    dma = pltpu.SemaphoreType.DMA
    vmem = pl.BlockSpec(memory_space=pltpu.VMEM)
    return pl.pallas_call(
        fused_kernel,
        out_shape=jax.ShapeDtypeStruct((2, ROWS, TW, HALF), BF16),
        in_specs=[
            pl.BlockSpec(memory_space=pltpu.SMEM), vmem, vmem, vmem,
            pl.BlockSpec(memory_space=pl.ANY), vmem,
        ],
        out_specs=vmem,
        scratch_shapes=[
            pltpu.VMEM((9, 4, IN, OUT), BF16),
            pltpu.VMEM((PARTS, 64, 128), BF16),
            pltpu.VMEM((PARTS, 64, 128), BF16),
            pltpu.VMEM((FRAMES, TILES * TW + 2 * RIM, ROWS, 128), F32),
            pltpu.VMEM((TILES, FRAMES + 2, WIN + 2, ROWS, 128), F32),
            pltpu.VMEM((TILES * FRAMES, ROWS, 128), F32),
            pltpu.VMEM((TILES * FRAMES, ROWS, 128), F32),
            pltpu.VMEM((TILES * FRAMES, ROWS, 128), F32),
            pltpu.VMEM((TILES, 2 * RIM, OUT), F32),
            pltpu.VMEM((FRAMES * WIN * ROWS, 9 * 128), BF16),
            pltpu.VMEM((FRAMES * WIN * ROWS, OUT), F32),
            pltpu.VMEM((TILES, 2 * block_rows, HALF), F32),
            pltpu.VMEM((TILES, 2 * block_rows, HALF), F32),
            pltpu.VMEM((TILES, 2 * block_rows, HALF), F32),
            pltpu.VMEM((TILES, block_rows, HALF), BF16),
            pltpu.VMEM((TILES, block_rows, HALF), BF16),
            pltpu.VMEM((TILES - 1, block_rows, HALF), BF16),
            pltpu.VMEM((TILES - 1, block_rows, HALF), BF16),
            dma((18,)), dma((PARTS - 1,)), dma((PARTS - 1,)),
            dma((TILES,)), dma((TILES,)), dma((TILES,)), dma((TILES,)),
            dma((TILES - 1,)), dma((TILES - 1,)),
        ],
        compiler_params=pltpu.CompilerParams(
            collective_id=0, has_side_effects=True, vmem_limit_bytes=48 * 2**20
        ),
    )(
        blend_profile, latent, norm_gain.reshape(1, HALF), norm_shift.reshape(1, HALF),
        kernel, conv_bias.reshape(1, HALF),
    )


def fits_fused(latent, kernel):
    sizes = tuple(lax.axis_size(axis) for axis in ("tile", "tm", "ch"))
    return (
        sizes == (TILES, BLOCKS, 2)
        and latent.shape == (2, ROWS, TW, HALF)
        and kernel.shape == (3, 3, 3, IN, OUT)
    )


def on_device(latent, norm_gain, norm_shift, kernel, conv_bias, blend_profile):
    arguments = (latent, norm_gain, norm_shift, kernel, conv_bias, blend_profile)
    if fits_fused(latent, kernel):
        return fused_on_device(*arguments)
    return gathered_on_device(*arguments)


def solution(mesh):
    in_specs = (
        P(("grp", "tm"), None, "tile", "ch"),
        P("ch"),
        P("ch"),
        P(None, None, None, ("ch", "tile", "tm"), None),
        P("ch"),
        P(),
    )
    out_specs = P(("grp", "tm"), None, "tile", "ch")
    return jax.shard_map(
        on_device, mesh=mesh, in_specs=in_specs, out_specs=out_specs, check_vma=False
    )
```

```python
import functools
import jax
import jax.numpy as jnp
from jax import lax
from jax.experimental import pallas as pl
from jax.experimental.pallas import tpu as pltpu
from jax.sharding import PartitionSpec as P

GROUPS = 32
RIM = 4


def with_halo(shard, sides, width):
    for axis, dim in sides:
        size, length = (lax.axis_size(axis), shard.shape[dim])
        up = [(i, (i + 1) % size) for i in range(size - 1)]
        down = [(j, i) for i, j in up]
        last = lax.slice_in_dim(shard, length - width, length, axis=dim)
        leading = lax.slice_in_dim(shard, 0, width, axis=dim)
        before = lax.ppermute(last, axis, up)
        after = lax.ppermute(leading, axis, down)
        shard = jnp.concatenate([before, shard, after], axis=dim)
    return shard


def passed_along(block, axis, distance):
    devices = range(lax.axis_size(axis))
    route = [(i - distance, i) for i in devices if i - distance in devices]
    return lax.ppermute(block, axis, route)


def ramp_weight(profile, position, margin):
    fraction = (position.astype(jnp.float32) + 0.5) / (2.0 * margin)
    exponent = 1.0 + profile.astype(jnp.float32)
    near_part = jnp.power(1.0 - fraction, exponent)
    far_part = jnp.power(fraction, exponent)
    return near_part / (near_part + far_part)


def frame_stats(values, colmask, groups):
    frame_count, row_count, col_count, chan_count = values.shape
    grouped = values.reshape(frame_count, row_count, col_count, groups, chan_count // groups)
    weight = colmask.reshape(1, 1, col_count, 1, 1)
    counted = row_count * (chan_count // groups) * jnp.sum(colmask)
    center = jnp.sum(grouped * weight, axis=(1, 2, 4)) / counted
    spread = (grouped - center[:, None, None, :, None]) * weight
    inverse = lax.rsqrt(jnp.sum(spread * spread, axis=(1, 2, 4)) / counted + 1e-06)
    return (center, inverse)


def activate(values, center, inverse, norm_gain, norm_shift, colmask, timemask, groups):
    frame_count, row_count, col_count, chan_count = values.shape
    grouped = values.reshape(frame_count, row_count, col_count, groups, chan_count // groups)
    normed = (grouped - center[:, None, None, :, None]) * inverse[:, None, None, :, None]
    normed = normed.reshape(values.shape) * norm_gain + norm_shift
    masked = jax.nn.silu(normed) * colmask[None, None, :, None] * timemask[:, None, None, None]
    return masked.astype(jnp.bfloat16)


def conv_taps(padded, kernel_part, frame_count, row_count, col_count):
    in_width = kernel_part.shape[3]
    running = None
    for tap_time in range(3):
        for tap_row in range(3):
            for tap_col in range(3):
                window = padded[
                    tap_time : tap_time + frame_count,
                    tap_row : tap_row + row_count,
                    tap_col : tap_col + col_count,
                ]
                contrib = jnp.dot(
                    window.reshape(-1, in_width),
                    kernel_part[tap_time, tap_row, tap_col],
                    preferred_element_type=jnp.float32,
                )
                running = contrib if running is None else running + contrib
    return running


def gathered_on_device(latent, norm_gain, norm_shift, kernel, conv_bias, blend_profile):
    frame_count, row_count, core_cols, chan_half = latent.shape
    out_chans = kernel.shape[4]
    groups = GROUPS // lax.axis_size("ch")
    ncols = core_cols + 2 * RIM
    tile_pos = lax.axis_index("tile")
    tile_count = lax.axis_size("tile")
    window_in = with_halo(latent, (("tile", 2),), RIM)
    cached = passed_along(window_in, "tm", 1)
    frames = jnp.concatenate([cached, window_in], axis=0).astype(jnp.float32)
    column = tile_pos * core_cols - RIM + jnp.arange(ncols, dtype=jnp.int32)
    colmask = ((column >= 0) & (column < tile_count * core_cols)).astype(jnp.float32)
    started = (lax.axis_index("tm") > 0).astype(jnp.float32)
    timemask = jnp.concatenate(
        [jnp.ones((2,), jnp.float32) * started, jnp.ones((frame_count,), jnp.float32)]
    )
    center, inverse = frame_stats(frames, colmask, groups)
    activated = activate(frames, center, inverse, norm_gain, norm_shift, colmask, timemask, groups)
    inputs = (jnp.pad(activated, ((0, 0), (1, 1), (1, 1), (0, 0))),)
    widths = (ncols,)

    def accumulate(shard_rows):
        return tuple(
            (
                conv_taps(source, shard_rows, frame_count, row_count, width_cols)
                for source, width_cols in zip(inputs, widths)
            )
        )

    totals = accumulate(lax.all_gather(kernel, ("tile", "tm"), axis=3, tiled=True))
    shaped = [
        running.reshape(frame_count, row_count, width_cols, out_chans)
        for running, width_cols in zip(totals, widths)
    ]
    joined = shaped[0]
    summed = lax.psum_scatter(joined, "ch", scatter_dimension=3, tiled=True)
    tile_out = (summed + conv_bias).astype(jnp.bfloat16)
    extended = with_halo(tile_out, (("tile", 2),), RIM)
    own_out = tile_out[:, :, RIM : RIM + core_cols]
    left_nbr = extended[:, :, :RIM]
    right_nbr = extended[:, :, ncols + RIM :]
    own_profile = lax.dynamic_index_in_dim(blend_profile, tile_pos, 0, keepdims=False)
    prev_profile = lax.dynamic_index_in_dim(
        blend_profile, jnp.maximum(tile_pos - 1, 0), 0, keepdims=False
    )
    offsets = jnp.arange(RIM, dtype=jnp.int32)
    left_weight = jnp.where(tile_pos > 0, ramp_weight(prev_profile, offsets + RIM, RIM), 0.0)
    right_weight = jnp.where(tile_pos < tile_count - 1, ramp_weight(own_profile, offsets, RIM), 1.0)
    left_wide = left_weight[None, None, :, None]
    right_wide = right_weight[None, None, :, None]
    own_float = own_out.astype(jnp.float32)
    head_cols = own_float[:, :, :RIM] * (1.0 - left_wide) + left_nbr.astype(jnp.float32) * left_wide
    tail_cols = own_float[:, :, core_cols - RIM :] * right_wide + right_nbr.astype(jnp.float32) * (
        1.0 - right_wide
    )
    middle = own_float[:, :, RIM : core_cols - RIM]
    return jnp.concatenate([head_cols, middle, tail_cols], axis=2).astype(jnp.bfloat16)


MESH = pl.DeviceIdType.MESH
TILES = 4
BLOCKS = 2
PARTS = TILES * BLOCKS
ROWS = 8
TW = 16
WIN = TW + 2 * RIM
IN = 32
FRAMES = 4
HALF = 256
OUT = 512
F32 = jnp.float32
BF16 = jnp.bfloat16


def iota(shape, dim):
    return lax.broadcasted_iota(jnp.int32, shape, dim)


def exact_dot(a, b):
    return jnp.dot(a, b, preferred_element_type=F32, precision=lax.Precision.HIGHEST)


def fused_kernel(
    profile_in, latent_in, gain_in, shift_in, kernel, bias_in, out,
    profile, latent, gain, shift, bias,
    weights, packed, arrived, grid, act, sums, centers, inverses, ramp, lhs, conv,
    keep, give, took, cross, crossed, send, landed,
    i_sem, w_sem, a_send, a_recv, s_send, s_recv, x_send, x_recv, z_send, z_recv,
):
    tile = lax.axis_index("tile")
    tm = lax.axis_index("tm")
    ch = lax.axis_index("ch")
    me = tile * BLOCKS + tm

    inputs = [
        pltpu.make_async_copy(source, target, i_sem.at[n])
        for n, (source, target) in enumerate(
            (
                (latent_in, latent), (profile_in, profile), (gain_in, gain),
                (shift_in, shift), (bias_in, bias),
            )
        )
    ]
    for load in inputs:
        load.start()
    loads = []
    for a in range(3):
        for e in range(3):
            for side in range(2):
                start = pl.multiple_of(((ch + side) % 2) * HALF, HALF)
                loads.append(
                    pltpu.make_async_copy(
                        kernel.at[a, :, e, :, pl.ds(start, HALF)],
                        weights.at[a * 3 + e, pl.ds(0, 3), :, pl.ds(side * HALF, HALF)],
                        w_sem.at[(a * 3 + e) * 2 + side],
                    )
                )
    for load in loads:
        load.start()

    barrier = pltpu.get_barrier_semaphore()
    for d in range(1, PARTS):
        j = (me + d) % PARTS
        pl.semaphore_signal(
            barrier, inc=1, device_id={"tile": j // BLOCKS, "tm": j % BLOCKS}, device_id_type=MESH
        )
    pl.semaphore_signal(barrier, inc=1, device_id={"ch": 1 - ch}, device_id_type=MESH)

    row_i, col_i = iota((128, 128), 0), iota((128, 128), 1)
    turn = jnp.where((row_i % ROWS) * TW + row_i // ROWS == col_i, 1.0, 0.0).astype(BF16)
    lane_block = iota((64, 128), 1) // IN
    inputs[0].wait()
    turned = [
        jnp.dot(turn, latent[f].reshape(ROWS * TW, HALF), preferred_element_type=F32)
        for f in range(2)
    ]
    for j in range(PARTS):
        lanes = slice((j // 4) * 128, (j // 4) * 128 + 128)
        joined = None
        for k in range(4):
            piece = turned[k // 2][(k % 2) * 64 : (k % 2) * 64 + 64, lanes]
            amount = ((k - j % 4) * IN) % 128
            if amount:
                piece = pltpu.roll(piece, amount, 1)
            joined = piece if joined is None else jnp.where(lane_block == k, piece, joined)
        packed[j] = joined.astype(BF16)

    pl.semaphore_wait(barrier, PARTS)
    moves = []
    for d in range(1, PARTS):
        j = (me + d) % PARTS
        moves.append(
            pltpu.make_async_remote_copy(
                src_ref=packed.at[j],
                dst_ref=arrived.at[me],
                send_sem=a_send.at[d - 1],
                recv_sem=a_recv.at[d - 1],
                device_id={"tile": j // BLOCKS, "tm": j % BLOCKS},
                device_id_type=MESH,
            )
        )
    for move in moves:
        move.start()
    arrived[me] = packed[me]

    act[:, 0:2] = jnp.zeros((TILES, 2, WIN + 2, ROWS, 128), F32)
    act[:, 2:, 0:1] = jnp.zeros((TILES, FRAMES, 1, ROWS, 128), F32)
    act[:, 2:, WIN + 1 :] = jnp.zeros((TILES, FRAMES, 1, ROWS, 128), F32)
    grid[:, 0:RIM] = jnp.zeros((FRAMES, RIM, ROWS, 128), F32)
    grid[:, RIM + TILES * TW :] = jnp.zeros((FRAMES, RIM, ROWS, 128), F32)
    weights[:, 3] = jnp.zeros((9, IN, OUT), BF16)
    for load in inputs[1:]:
        load.wait()
    fraction = (iota((8, OUT), 0).astype(F32) + 0.5) / (2.0 * RIM)
    for margin in range(TILES):
        p = jnp.full((8, OUT), profile[margin], jnp.int32)
        near, far = 1.0 - fraction, fraction
        near_part, far_part = near, far
        for power in range(1, 4):
            near_part = jnp.where(p >= power, near_part * near, near_part)
            far_part = jnp.where(p >= power, far_part * far, far_part)
        ramp[margin] = near_part / (near_part + far_part)
    pick = jnp.where(iota((HALF, 128), 0) == me * IN + iota((HALF, 128), 1) % IN, 1.0, 0.0)
    own_gain = exact_dot(jnp.broadcast_to(gain[...], (8, HALF)), pick)
    own_shift = exact_dot(jnp.broadcast_to(shift[...], (8, HALF)), pick)
    group = jnp.where(
        (row_i // (IN // 2)) == (col_i // (IN // 2)), 1.0, 0.0
    )
    spread = [
        jnp.where((row_i // IN == k) & (row_i % IN == col_i % IN), 1.0, 0.0).astype(BF16)
        for k in range(4)
    ]

    for move in moves:
        move.wait()
    everything = arrived[...].reshape(PARTS * 64, 128)
    for k in range(4):
        wide = jnp.dot(everything, spread[k], preferred_element_type=F32)
        for s in range(PARTS):
            first = RIM + (s // BLOCKS) * TW + (k % 2) * (TW // 2)
            grid[(s % BLOCKS) * 2 + k // 2, first : first + TW // 2] = wide[
                s * 64 : s * 64 + 64
            ].reshape(TW // 2, ROWS, 128)

    def present(t):
        column = t * TW + iota((WIN, ROWS, 128), 0)
        return jnp.where((column >= RIM) & (column < RIM + TILES * TW), 1.0, 0.0)

    def totals(n, _):
        t, f = n // FRAMES, n % FRAMES
        sums[n] = jnp.sum(grid[f, pl.ds(t * TW, WIN)], axis=0)
        return 0

    pairs = TILES * FRAMES
    tile_of = iota((pairs, 1, 128), 0) // FRAMES
    counted = jnp.where((tile_of == 0) | (tile_of == TILES - 1), WIN - RIM, WIN).astype(F32)
    counted = counted * float(ROWS * (IN // 2))
    lax.fori_loop(0, pairs, totals, 0)

    def grouped():
        per_group = exact_dot(sums[...].reshape(pairs * ROWS, 128), group)
        return jnp.sum(per_group.reshape(pairs, ROWS, 128), axis=1, keepdims=True) / counted

    centers[...] = jnp.broadcast_to(grouped(), (pairs, ROWS, 128))

    def squares(n, _):
        t, f = n // FRAMES, n % FRAMES
        apart = (grid[f, pl.ds(t * TW, WIN)] - centers[n]) * present(t)
        sums[n] = jnp.sum(apart * apart, axis=0)
        return 0

    lax.fori_loop(0, pairs, squares, 0)
    inverses[...] = jnp.broadcast_to(lax.rsqrt(grouped() + 1e-06), (pairs, ROWS, 128))

    block_of, row_of = iota((ROWS, 128), 1) // IN, iota((ROWS, 128), 0)
    inside = (block_of == 1) | ((block_of == 0) & (row_of > 0))
    inside = jnp.where(inside | ((block_of == 2) & (row_of < ROWS - 1)), 1.0, 0.0)

    def activate_window(n, _):
        t, f = n // FRAMES, n % FRAMES
        v = (grid[f, pl.ds(t * TW, WIN)] - centers[n]) * inverses[n] * own_gain + own_shift
        v = v / (1.0 + jnp.exp(-v)) * present(t)
        before, after = pltpu.roll(v, 1, 1), pltpu.roll(v, ROWS - 1, 1)
        v = jnp.where(block_of == 0, before, jnp.where(block_of == 2, after, v))
        act[t, f + 2, 1 : WIN + 1] = v * inside
        return 0

    lax.fori_loop(0, pairs, activate_window, 0)
    for load in loads:
        load.wait()

    rows_kept = FRAMES * TW * ROWS
    block_rows = rows_kept // BLOCKS

    def target(i):
        upper = 1 - i // 2
        lower = ((i + 1) // 2) % 2
        return 2 * ((tile // 2 + upper) % 2) + (tile % 2 + lower) % 2

    def next_stop(i):
        later = (i + 1) // 2
        later = later - later // 2
        return later * target(i) + (1 - later) * (2 * tile + 1 - 5 * (tile // 2))

    inner = (tile == 1) | (tile == 2)

    def sibling_copy(i):
        return pltpu.make_async_remote_copy(
            src_ref=give.at[i], dst_ref=took.at[i],
            send_sem=s_send.at[i], recv_sem=s_recv.at[i],
            device_id={"ch": 1 - ch}, device_id_type=MESH,
        )

    def cross_copy(i):
        return pltpu.make_async_remote_copy(
            src_ref=cross.at[i], dst_ref=crossed.at[i],
            send_sem=x_send.at[i], recv_sem=x_recv.at[i],
            device_id={"tm": 1 - tm}, device_id_type=MESH,
        )

    def owner_copy(i):
        return pltpu.make_async_remote_copy(
            src_ref=send.at[i], dst_ref=landed.at[i],
            send_sem=z_send.at[i], recv_sem=z_recv.at[i],
            device_id={"tile": next_stop(i)}, device_id_type=MESH,
        )

    own_rows = pl.ds(pl.multiple_of(tm * block_rows, block_rows), block_rows)
    other_rows = pl.ds(pl.multiple_of((1 - tm) * block_rows, block_rows), block_rows)

    def convolve(i):
        t = target(i)
        left, right = (t + TILES - 1) % TILES, (t + 1) % TILES
        for f in range(FRAMES):
            for a in range(3):
                for e in range(3):
                    lanes = slice((a * 3 + e) * 128, (a * 3 + e) * 128 + 128)
                    row = f * WIN * ROWS
                    for owner, first, count in (
                        (t, RIM, TW), (left, TW + RIM, RIM), (right, 0, RIM),
                    ):
                        piece = act[owner, f + a, first + e : first + e + count]
                        lhs[row : row + count * ROWS, lanes] = piece.reshape(
                            count * ROWS, 128
                        ).astype(BF16)
                        row += count * ROWS
        conv[...] = jnp.dot(
            lhs[...], weights[...].reshape(9 * 128, OUT), preferred_element_type=F32
        )
        has_left = jnp.where(t > 0, 1.0, 0.0)
        has_right = jnp.where(t < TILES - 1, 1.0, 0.0)
        for f in range(FRAMES):
            base = f * WIN * ROWS
            for c in range(TW):
                value = conv[base + c * ROWS : base + (c + 1) * ROWS]
                if c < RIM:
                    w = ramp[left, RIM + c : RIM + c + 1] * has_left
                    far = base + (TW + c) * ROWS
                    value = value * (1.0 - w) + conv[far : far + ROWS] * w
                if c >= TW - RIM:
                    j = c - (TW - RIM)
                    w = 1.0 - (1.0 - ramp[t, j : j + 1]) * has_right
                    far = base + (TW + RIM + j) * ROWS
                    value = value * w + conv[far : far + ROWS] * (1.0 - w)
                row = (f * TW + c) * ROWS
                keep[i, row : row + ROWS] = value[:, :HALF]
                give[i, row : row + ROWS] = value[:, HALF:]
        sibling_copy(i).start()

    def join_sibling(i):
        sibling_copy(i).wait_recv()
        cross[i] = (keep[i, other_rows] + took[i, other_rows]).astype(BF16)
        cross_copy(i).start()

    def join_cross(i):
        cross_copy(i).wait_recv()
        return keep[i, own_rows] + took[i, own_rows] + crossed[i].astype(F32)

    def pass_on(i):
        value = join_cross(i)
        send[i] = value.astype(BF16)

        @pl.when((i == 1) & inner)
        def _():
            owner_copy(0).wait_recv()
            send[i] = (value + landed[0].astype(F32)).astype(BF16)

        owner_copy(i).start()

    def step(s, _):
        pl.when(s < TILES)(lambda: convolve(s))
        pl.when((s >= 1) & (s <= TILES))(lambda: join_sibling(s - 1))
        pl.when((s >= 2) & (s <= TILES))(lambda: pass_on(s - 2))
        return 0

    lax.fori_loop(0, TILES + 1, step, 0)
    total = join_cross(TILES - 1)

    @pl.when(jnp.logical_not(inner))
    def _():
        owner_copy(0).wait_recv()

    total = total + jnp.where(inner, 0.0, landed[0].astype(F32))
    for i in range(1, TILES - 1):
        owner_copy(i).wait_recv()
        total = total + landed[i].astype(F32)
    result = (total + bias[...]).astype(BF16)
    back = jnp.where((row_i % TW) * ROWS + row_i // TW == col_i, 1.0, 0.0).astype(BF16)
    for f in range(2):
        frame = result[f * TW * ROWS : (f + 1) * TW * ROWS]
        out[f] = (
            jnp.dot(back, frame, preferred_element_type=F32)
            .astype(BF16)
            .reshape(ROWS, TW, HALF)
        )
    for i in range(TILES):
        sibling_copy(i).wait_send()
        cross_copy(i).wait_send()
        if i < TILES - 1:
            owner_copy(i).wait_send()


def fused_on_device(latent, norm_gain, norm_shift, kernel, conv_bias, blend_profile):
    block_rows = 2 * TW * ROWS
    dma = pltpu.SemaphoreType.DMA
    hbm = pl.BlockSpec(memory_space=pltpu.MemorySpace.HBM)
    vector = pltpu.VMEM((1, HALF), F32)
    return pl.pallas_call(
        fused_kernel,
        out_shape=jax.ShapeDtypeStruct((2, ROWS, TW, HALF), BF16),
        in_specs=[hbm] * 6,
        out_specs=pl.BlockSpec(memory_space=pltpu.VMEM),
        scratch_shapes=[
            pltpu.SMEM((TILES,), jnp.int32),
            pltpu.VMEM((2, ROWS, TW, HALF), BF16),
            vector, vector, vector,
            pltpu.VMEM((9, 4, IN, OUT), BF16),
            pltpu.VMEM((PARTS, 64, 128), BF16),
            pltpu.VMEM((PARTS, 64, 128), BF16),
            pltpu.VMEM((FRAMES, TILES * TW + 2 * RIM, ROWS, 128), F32),
            pltpu.VMEM((TILES, FRAMES + 2, WIN + 2, ROWS, 128), F32),
            pltpu.VMEM((TILES * FRAMES, ROWS, 128), F32),
            pltpu.VMEM((TILES * FRAMES, ROWS, 128), F32),
            pltpu.VMEM((TILES * FRAMES, ROWS, 128), F32),
            pltpu.VMEM((TILES, 2 * RIM, OUT), F32),
            pltpu.VMEM((FRAMES * WIN * ROWS, 9 * 128), BF16),
            pltpu.VMEM((FRAMES * WIN * ROWS, OUT), F32),
            pltpu.VMEM((TILES, 2 * block_rows, HALF), F32),
            pltpu.VMEM((TILES, 2 * block_rows, HALF), F32),
            pltpu.VMEM((TILES, 2 * block_rows, HALF), F32),
            pltpu.VMEM((TILES, block_rows, HALF), BF16),
            pltpu.VMEM((TILES, block_rows, HALF), BF16),
            pltpu.VMEM((TILES - 1, block_rows, HALF), BF16),
            pltpu.VMEM((TILES - 1, block_rows, HALF), BF16),
            dma((5,)), dma((18,)), dma((PARTS - 1,)), dma((PARTS - 1,)),
            dma((TILES,)), dma((TILES,)), dma((TILES,)), dma((TILES,)),
            dma((TILES - 1,)), dma((TILES - 1,)),
        ],
        compiler_params=pltpu.CompilerParams(
            collective_id=0, has_side_effects=True, vmem_limit_bytes=63 * 2**20
        ),
    )(
        blend_profile, latent, norm_gain.reshape(1, HALF), norm_shift.reshape(1, HALF),
        kernel, conv_bias.reshape(1, HALF),
    )


def fits_fused(latent, kernel):
    sizes = tuple(lax.axis_size(axis) for axis in ("tile", "tm", "ch"))
    return (
        sizes == (TILES, BLOCKS, 2)
        and latent.shape == (2, ROWS, TW, HALF)
        and kernel.shape == (3, 3, 3, IN, OUT)
    )


def on_device(latent, norm_gain, norm_shift, kernel, conv_bias, blend_profile):
    arguments = (latent, norm_gain, norm_shift, kernel, conv_bias, blend_profile)
    if fits_fused(latent, kernel):
        return fused_on_device(*arguments)
    return gathered_on_device(*arguments)


def solution(mesh):
    in_specs = (
        P(("grp", "tm"), None, "tile", "ch"),
        P("ch"),
        P("ch"),
        P(None, None, None, ("ch", "tile", "tm"), None),
        P("ch"),
        P(),
    )
    out_specs = P(("grp", "tm"), None, "tile", "ch")
    return jax.shard_map(
        on_device, mesh=mesh, in_specs=in_specs, out_specs=out_specs, check_vma=False
    )
```

```python
import functools
import jax
import jax.numpy as jnp
from jax import lax
from jax.experimental import pallas as pl
from jax.experimental.pallas import tpu as pltpu
from jax.sharding import PartitionSpec as P

GROUPS = 32
RIM = 4


def with_halo(shard, sides, width):
    for axis, dim in sides:
        size, length = (lax.axis_size(axis), shard.shape[dim])
        up = [(i, (i + 1) % size) for i in range(size - 1)]
        down = [(j, i) for i, j in up]
        last = lax.slice_in_dim(shard, length - width, length, axis=dim)
        leading = lax.slice_in_dim(shard, 0, width, axis=dim)
        before = lax.ppermute(last, axis, up)
        after = lax.ppermute(leading, axis, down)
        shard = jnp.concatenate([before, shard, after], axis=dim)
    return shard


def passed_along(block, axis, distance):
    devices = range(lax.axis_size(axis))
    route = [(i - distance, i) for i in devices if i - distance in devices]
    return lax.ppermute(block, axis, route)


def ramp_weight(profile, position, margin):
    fraction = (position.astype(jnp.float32) + 0.5) / (2.0 * margin)
    exponent = 1.0 + profile.astype(jnp.float32)
    near_part = jnp.power(1.0 - fraction, exponent)
    far_part = jnp.power(fraction, exponent)
    return near_part / (near_part + far_part)


def frame_stats(values, colmask, groups):
    frame_count, row_count, col_count, chan_count = values.shape
    grouped = values.reshape(frame_count, row_count, col_count, groups, chan_count // groups)
    weight = colmask.reshape(1, 1, col_count, 1, 1)
    counted = row_count * (chan_count // groups) * jnp.sum(colmask)
    center = jnp.sum(grouped * weight, axis=(1, 2, 4)) / counted
    spread = (grouped - center[:, None, None, :, None]) * weight
    inverse = lax.rsqrt(jnp.sum(spread * spread, axis=(1, 2, 4)) / counted + 1e-06)
    return (center, inverse)


def activate(values, center, inverse, norm_gain, norm_shift, colmask, timemask, groups):
    frame_count, row_count, col_count, chan_count = values.shape
    grouped = values.reshape(frame_count, row_count, col_count, groups, chan_count // groups)
    normed = (grouped - center[:, None, None, :, None]) * inverse[:, None, None, :, None]
    normed = normed.reshape(values.shape) * norm_gain + norm_shift
    masked = jax.nn.silu(normed) * colmask[None, None, :, None] * timemask[:, None, None, None]
    return masked.astype(jnp.bfloat16)


def conv_taps(padded, kernel_part, frame_count, row_count, col_count):
    in_width = kernel_part.shape[3]
    running = None
    for tap_time in range(3):
        for tap_row in range(3):
            for tap_col in range(3):
                window = padded[
                    tap_time : tap_time + frame_count,
                    tap_row : tap_row + row_count,
                    tap_col : tap_col + col_count,
                ]
                contrib = jnp.dot(
                    window.reshape(-1, in_width),
                    kernel_part[tap_time, tap_row, tap_col],
                    preferred_element_type=jnp.float32,
                )
                running = contrib if running is None else running + contrib
    return running


def gathered_on_device(latent, norm_gain, norm_shift, kernel, conv_bias, blend_profile):
    frame_count, row_count, core_cols, chan_half = latent.shape
    out_chans = kernel.shape[4]
    groups = GROUPS // lax.axis_size("ch")
    ncols = core_cols + 2 * RIM
    tile_pos = lax.axis_index("tile")
    tile_count = lax.axis_size("tile")
    window_in = with_halo(latent, (("tile", 2),), RIM)
    cached = passed_along(window_in, "tm", 1)
    frames = jnp.concatenate([cached, window_in], axis=0).astype(jnp.float32)
    column = tile_pos * core_cols - RIM + jnp.arange(ncols, dtype=jnp.int32)
    colmask = ((column >= 0) & (column < tile_count * core_cols)).astype(jnp.float32)
    started = (lax.axis_index("tm") > 0).astype(jnp.float32)
    timemask = jnp.concatenate(
        [jnp.ones((2,), jnp.float32) * started, jnp.ones((frame_count,), jnp.float32)]
    )
    center, inverse = frame_stats(frames, colmask, groups)
    activated = activate(frames, center, inverse, norm_gain, norm_shift, colmask, timemask, groups)
    inputs = (jnp.pad(activated, ((0, 0), (1, 1), (1, 1), (0, 0))),)
    widths = (ncols,)

    def accumulate(shard_rows):
        return tuple(
            (
                conv_taps(source, shard_rows, frame_count, row_count, width_cols)
                for source, width_cols in zip(inputs, widths)
            )
        )

    totals = accumulate(lax.all_gather(kernel, ("tile", "tm"), axis=3, tiled=True))
    shaped = [
        running.reshape(frame_count, row_count, width_cols, out_chans)
        for running, width_cols in zip(totals, widths)
    ]
    joined = shaped[0]
    summed = lax.psum_scatter(joined, "ch", scatter_dimension=3, tiled=True)
    tile_out = (summed + conv_bias).astype(jnp.bfloat16)
    extended = with_halo(tile_out, (("tile", 2),), RIM)
    own_out = tile_out[:, :, RIM : RIM + core_cols]
    left_nbr = extended[:, :, :RIM]
    right_nbr = extended[:, :, ncols + RIM :]
    own_profile = lax.dynamic_index_in_dim(blend_profile, tile_pos, 0, keepdims=False)
    prev_profile = lax.dynamic_index_in_dim(
        blend_profile, jnp.maximum(tile_pos - 1, 0), 0, keepdims=False
    )
    offsets = jnp.arange(RIM, dtype=jnp.int32)
    left_weight = jnp.where(tile_pos > 0, ramp_weight(prev_profile, offsets + RIM, RIM), 0.0)
    right_weight = jnp.where(tile_pos < tile_count - 1, ramp_weight(own_profile, offsets, RIM), 1.0)
    left_wide = left_weight[None, None, :, None]
    right_wide = right_weight[None, None, :, None]
    own_float = own_out.astype(jnp.float32)
    head_cols = own_float[:, :, :RIM] * (1.0 - left_wide) + left_nbr.astype(jnp.float32) * left_wide
    tail_cols = own_float[:, :, core_cols - RIM :] * right_wide + right_nbr.astype(jnp.float32) * (
        1.0 - right_wide
    )
    middle = own_float[:, :, RIM : core_cols - RIM]
    return jnp.concatenate([head_cols, middle, tail_cols], axis=2).astype(jnp.bfloat16)


MESH = pl.DeviceIdType.MESH
TILES = 4
BLOCKS = 2
PARTS = TILES * BLOCKS
ROWS = 8
TW = 16
WIN = TW + 2 * RIM
IN = 32
FRAMES = 4
HALF = 256
OUT = 512
F32 = jnp.float32
BF16 = jnp.bfloat16


def iota(shape, dim):
    return lax.broadcasted_iota(jnp.int32, shape, dim)


def exact_dot(a, b):
    return jnp.dot(a, b, preferred_element_type=F32, precision=lax.Precision.HIGHEST)


def fused_kernel(
    profile_in, latent_in, gain_in, shift_in, kernel, bias_in, out,
    profile, latent, gain, shift, bias,
    weights, packed, arrived, grid, act, sums, centers, inverses, ramp, lhs, conv,
    keep, give, took, cross, crossed, send, landed,
    i_sem, w_sem, a_send, a_recv, s_send, s_recv, x_send, x_recv, z_send, z_recv,
):
    tile = lax.axis_index("tile")
    tm = lax.axis_index("tm")
    ch = lax.axis_index("ch")
    me = tile * BLOCKS + tm

    inputs = [
        pltpu.make_async_copy(source, target, i_sem.at[n])
        for n, (source, target) in enumerate(
            (
                (latent_in, latent), (profile_in, profile), (gain_in, gain),
                (shift_in, shift), (bias_in, bias),
            )
        )
    ]
    for load in inputs:
        load.start()
    loads = []
    for a in range(3):
        for e in range(3):
            for side in range(2):
                start = pl.multiple_of(((ch + side) % 2) * HALF, HALF)
                loads.append(
                    pltpu.make_async_copy(
                        kernel.at[a, :, e, :, pl.ds(start, HALF)],
                        weights.at[a * 3 + e, pl.ds(0, 3), :, pl.ds(side * HALF, HALF)],
                        w_sem.at[(a * 3 + e) * 2 + side],
                    )
                )
    for load in loads:
        load.start()

    barrier = pltpu.get_barrier_semaphore()
    for d in range(1, PARTS):
        j = (me + d) % PARTS
        pl.semaphore_signal(
            barrier, inc=1, device_id={"tile": j // BLOCKS, "tm": j % BLOCKS}, device_id_type=MESH
        )
    pl.semaphore_signal(barrier, inc=1, device_id={"ch": 1 - ch}, device_id_type=MESH)

    row_i, col_i = iota((128, 128), 0), iota((128, 128), 1)
    turn = jnp.where((row_i % ROWS) * TW + row_i // ROWS == col_i, 1.0, 0.0).astype(BF16)
    lane_block = iota((64, 128), 1) // IN
    inputs[0].wait()
    turned = [
        jnp.dot(turn, latent[f].reshape(ROWS * TW, HALF), preferred_element_type=F32)
        for f in range(2)
    ]
    for j in range(PARTS):
        lanes = slice((j // 4) * 128, (j // 4) * 128 + 128)
        joined = None
        for k in range(4):
            piece = turned[k // 2][(k % 2) * 64 : (k % 2) * 64 + 64, lanes]
            amount = ((k - j % 4) * IN) % 128
            if amount:
                piece = pltpu.roll(piece, amount, 1)
            joined = piece if joined is None else jnp.where(lane_block == k, piece, joined)
        packed[j] = joined.astype(BF16)

    pl.semaphore_wait(barrier, PARTS)
    moves = []
    for d in range(1, PARTS):
        j = (me + d) % PARTS
        moves.append(
            pltpu.make_async_remote_copy(
                src_ref=packed.at[j],
                dst_ref=arrived.at[me],
                send_sem=a_send.at[d - 1],
                recv_sem=a_recv.at[d - 1],
                device_id={"tile": j // BLOCKS, "tm": j % BLOCKS},
                device_id_type=MESH,
            )
        )
    for move in moves:
        move.start()
    arrived[me] = packed[me]

    act[:, 0:2] = jnp.zeros((TILES, 2, WIN + 2, ROWS, 128), F32)
    act[:, 2:, 0:1] = jnp.zeros((TILES, FRAMES, 1, ROWS, 128), F32)
    act[:, 2:, WIN + 1 :] = jnp.zeros((TILES, FRAMES, 1, ROWS, 128), F32)
    grid[:, 0:RIM] = jnp.zeros((FRAMES, RIM, ROWS, 128), F32)
    grid[:, RIM + TILES * TW :] = jnp.zeros((FRAMES, RIM, ROWS, 128), F32)
    weights[:, 3] = jnp.zeros((9, IN, OUT), BF16)
    for load in inputs[1:]:
        load.wait()
    fraction = (iota((8, OUT), 0).astype(F32) + 0.5) / (2.0 * RIM)
    for margin in range(TILES):
        p = jnp.full((8, OUT), profile[margin], jnp.int32)
        near, far = 1.0 - fraction, fraction
        near_part, far_part = near, far
        for power in range(1, 4):
            near_part = jnp.where(p >= power, near_part * near, near_part)
            far_part = jnp.where(p >= power, far_part * far, far_part)
        ramp[margin] = near_part / (near_part + far_part)
    pick = jnp.where(iota((HALF, 128), 0) == me * IN + iota((HALF, 128), 1) % IN, 1.0, 0.0)
    own_gain = exact_dot(jnp.broadcast_to(gain[...], (8, HALF)), pick)
    own_shift = exact_dot(jnp.broadcast_to(shift[...], (8, HALF)), pick)
    group = jnp.where(
        (row_i // (IN // 2)) == (col_i // (IN // 2)), 1.0, 0.0
    )
    spread = [
        jnp.where((row_i // IN == k) & (row_i % IN == col_i % IN), 1.0, 0.0).astype(BF16)
        for k in range(4)
    ]

    for move in moves:
        move.wait()
    everything = arrived[...].reshape(PARTS * 64, 128)
    for k in range(4):
        wide = jnp.dot(everything, spread[k], preferred_element_type=F32)
        for s in range(PARTS):
            first = RIM + (s // BLOCKS) * TW + (k % 2) * (TW // 2)
            grid[(s % BLOCKS) * 2 + k // 2, first : first + TW // 2] = wide[
                s * 64 : s * 64 + 64
            ].reshape(TW // 2, ROWS, 128)

    def present(t):
        column = t * TW + iota((WIN, ROWS, 128), 0)
        return jnp.where((column >= RIM) & (column < RIM + TILES * TW), 1.0, 0.0)

    def totals(n, _):
        t, f = n // FRAMES, n % FRAMES
        sums[n] = jnp.sum(grid[f, pl.ds(t * TW, WIN)], axis=0)
        return 0

    pairs = TILES * FRAMES
    tile_of = iota((pairs, 1, 128), 0) // FRAMES
    counted = jnp.where((tile_of == 0) | (tile_of == TILES - 1), WIN - RIM, WIN).astype(F32)
    counted = counted * float(ROWS * (IN // 2))
    lax.fori_loop(0, pairs, totals, 0)

    def grouped():
        per_group = exact_dot(sums[...].reshape(pairs * ROWS, 128), group)
        return jnp.sum(per_group.reshape(pairs, ROWS, 128), axis=1, keepdims=True) / counted

    centers[...] = jnp.broadcast_to(grouped(), (pairs, ROWS, 128))

    def squares(n, _):
        t, f = n // FRAMES, n % FRAMES
        apart = (grid[f, pl.ds(t * TW, WIN)] - centers[n]) * present(t)
        sums[n] = jnp.sum(apart * apart, axis=0)
        return 0

    lax.fori_loop(0, pairs, squares, 0)
    inverses[...] = jnp.broadcast_to(lax.rsqrt(grouped() + 1e-06), (pairs, ROWS, 128))

    block_of, row_of = iota((ROWS, 128), 1) // IN, iota((ROWS, 128), 0)
    inside = (block_of == 1) | ((block_of == 0) & (row_of > 0))
    inside = jnp.where(inside | ((block_of == 2) & (row_of < ROWS - 1)), 1.0, 0.0)

    def activate_window(n, _):
        t, f = n // FRAMES, n % FRAMES
        v = (grid[f, pl.ds(t * TW, WIN)] - centers[n]) * inverses[n] * own_gain + own_shift
        v = v / (1.0 + jnp.exp(-v)) * present(t)
        before, after = pltpu.roll(v, 1, 1), pltpu.roll(v, ROWS - 1, 1)
        v = jnp.where(block_of == 0, before, jnp.where(block_of == 2, after, v))
        act[t, f + 2, 1 : WIN + 1] = v * inside
        return 0

    lax.fori_loop(0, pairs, activate_window, 0)
    for load in loads:
        load.wait()

    def target(i):
        upper = 1 - i // 2
        lower = ((i + 1) // 2) % 2
        return 2 * ((tile // 2 + upper) % 2) + (tile % 2 + lower) % 2

    def next_stop(i):
        later = (i + 1) // 2
        later = later - later // 2
        return later * target(i) + (1 - later) * (2 * tile + 1 - 5 * (tile // 2))

    inner = (tile == 1) | (tile == 2)

    def sibling_copy(i, part):
        return pltpu.make_async_remote_copy(
            src_ref=give.at[i, part], dst_ref=took.at[i, part],
            send_sem=s_send.at[i * 2 + part], recv_sem=s_recv.at[i * 2 + part],
            device_id={"ch": 1 - ch}, device_id_type=MESH,
        )

    def cross_copy(i):
        return pltpu.make_async_remote_copy(
            src_ref=cross.at[i], dst_ref=crossed.at[i],
            send_sem=x_send.at[i], recv_sem=x_recv.at[i],
            device_id={"tm": 1 - tm}, device_id_type=MESH,
        )

    def owner_copy(i):
        return pltpu.make_async_remote_copy(
            src_ref=send.at[i], dst_ref=landed.at[i],
            send_sem=z_send.at[i], recv_sem=z_recv.at[i],
            device_id={"tile": next_stop(i)}, device_id_type=MESH,
        )

    def convolve(i, part):
        start = ((tm + 1 + part) % BLOCKS) * 2
        t = target(i)
        left, right = (t + TILES - 1) % TILES, (t + 1) % TILES
        for f in range(2):
            for a in range(3):
                for e in range(3):
                    lanes = slice((a * 3 + e) * 128, (a * 3 + e) * 128 + 128)
                    row = f * WIN * ROWS
                    for owner, first, count in (
                        (t, RIM, TW), (left, TW + RIM, RIM), (right, 0, RIM),
                    ):
                        piece = act[owner, start + f + a, first + e : first + e + count]
                        lhs[row : row + count * ROWS, lanes] = piece.reshape(
                            count * ROWS, 128
                        ).astype(BF16)
                        row += count * ROWS
        conv[...] = jnp.dot(
            lhs[...], weights[...].reshape(9 * 128, OUT), preferred_element_type=F32
        )
        has_left = jnp.where(t > 0, 1.0, 0.0)
        has_right = jnp.where(t < TILES - 1, 1.0, 0.0)
        for f in range(2):
            base = f * WIN * ROWS
            for c in range(TW):
                value = conv[base + c * ROWS : base + (c + 1) * ROWS]
                if c < RIM:
                    w = ramp[left, RIM + c : RIM + c + 1] * has_left
                    far = base + (TW + c) * ROWS
                    value = value * (1.0 - w) + conv[far : far + ROWS] * w
                if c >= TW - RIM:
                    j = c - (TW - RIM)
                    w = 1.0 - (1.0 - ramp[t, j : j + 1]) * has_right
                    far = base + (TW + RIM + j) * ROWS
                    value = value * w + conv[far : far + ROWS] * (1.0 - w)
                row = (f * TW + c) * ROWS
                keep[i, part, row : row + ROWS] = value[:, :HALF]
                give[i, part, row : row + ROWS] = value[:, HALF:]
        sibling_copy(i, part).start()

    def join_sibling(i):
        sibling_copy(i, 0).wait_recv()
        cross[i] = (keep[i, 0] + took[i, 0]).astype(BF16)
        cross_copy(i).start()

    def join_cross(i):
        sibling_copy(i, 1).wait_recv()
        cross_copy(i).wait_recv()
        return keep[i, 1] + took[i, 1] + crossed[i].astype(F32)

    def pass_on(i):
        value = join_cross(i)
        send[i] = value.astype(BF16)

        @pl.when((i == 1) & inner)
        def _():
            owner_copy(0).wait_recv()
            send[i] = (value + landed[0].astype(F32)).astype(BF16)

        owner_copy(i).start()

    def step(s, _):
        convolve(s, 0)
        convolve(s, 1)
        join_sibling(s)
        pl.when(s >= 1)(lambda: pass_on(s - 1))
        return 0

    lax.fori_loop(0, TILES, step, 0)
    total = join_cross(TILES - 1)

    @pl.when(jnp.logical_not(inner))
    def _():
        owner_copy(0).wait_recv()

    total = total + jnp.where(inner, 0.0, landed[0].astype(F32))
    for i in range(1, TILES - 1):
        owner_copy(i).wait_recv()
        total = total + landed[i].astype(F32)
    result = (total + bias[...]).astype(BF16)
    back = jnp.where((row_i % TW) * ROWS + row_i // TW == col_i, 1.0, 0.0).astype(BF16)
    for f in range(2):
        frame = result[f * TW * ROWS : (f + 1) * TW * ROWS]
        out[f] = (
            jnp.dot(back, frame, preferred_element_type=F32)
            .astype(BF16)
            .reshape(ROWS, TW, HALF)
        )
    for i in range(TILES):
        sibling_copy(i, 0).wait_send()
        sibling_copy(i, 1).wait_send()
        cross_copy(i).wait_send()
        if i < TILES - 1:
            owner_copy(i).wait_send()


def fused_on_device(latent, norm_gain, norm_shift, kernel, conv_bias, blend_profile):
    block_rows = 2 * TW * ROWS
    dma = pltpu.SemaphoreType.DMA
    hbm = pl.BlockSpec(memory_space=pltpu.MemorySpace.HBM)
    vector = pltpu.VMEM((1, HALF), F32)
    return pl.pallas_call(
        fused_kernel,
        out_shape=jax.ShapeDtypeStruct((2, ROWS, TW, HALF), BF16),
        in_specs=[hbm] * 6,
        out_specs=pl.BlockSpec(memory_space=pltpu.VMEM),
        scratch_shapes=[
            pltpu.SMEM((TILES,), jnp.int32),
            pltpu.VMEM((2, ROWS, TW, HALF), BF16),
            vector, vector, vector,
            pltpu.VMEM((9, 4, IN, OUT), BF16),
            pltpu.VMEM((PARTS, 64, 128), BF16),
            pltpu.VMEM((PARTS, 64, 128), BF16),
            pltpu.VMEM((FRAMES, TILES * TW + 2 * RIM, ROWS, 128), F32),
            pltpu.VMEM((TILES, FRAMES + 2, WIN + 2, ROWS, 128), F32),
            pltpu.VMEM((TILES * FRAMES, ROWS, 128), F32),
            pltpu.VMEM((TILES * FRAMES, ROWS, 128), F32),
            pltpu.VMEM((TILES * FRAMES, ROWS, 128), F32),
            pltpu.VMEM((TILES, 2 * RIM, OUT), F32),
            pltpu.VMEM((2 * WIN * ROWS, 9 * 128), BF16),
            pltpu.VMEM((2 * WIN * ROWS, OUT), F32),
            pltpu.VMEM((TILES, 2, block_rows, HALF), F32),
            pltpu.VMEM((TILES, 2, block_rows, HALF), F32),
            pltpu.VMEM((TILES, 2, block_rows, HALF), F32),
            pltpu.VMEM((TILES, block_rows, HALF), BF16),
            pltpu.VMEM((TILES, block_rows, HALF), BF16),
            pltpu.VMEM((TILES - 1, block_rows, HALF), BF16),
            pltpu.VMEM((TILES - 1, block_rows, HALF), BF16),
            dma((5,)), dma((18,)), dma((PARTS - 1,)), dma((PARTS - 1,)),
            dma((2 * TILES,)), dma((2 * TILES,)), dma((TILES,)), dma((TILES,)),
            dma((TILES - 1,)), dma((TILES - 1,)),
        ],
        compiler_params=pltpu.CompilerParams(
            collective_id=0, has_side_effects=True, vmem_limit_bytes=63 * 2**20
        ),
    )(
        blend_profile, latent, norm_gain.reshape(1, HALF), norm_shift.reshape(1, HALF),
        kernel, conv_bias.reshape(1, HALF),
    )


def fits_fused(latent, kernel):
    sizes = tuple(lax.axis_size(axis) for axis in ("tile", "tm", "ch"))
    return (
        sizes == (TILES, BLOCKS, 2)
        and latent.shape == (2, ROWS, TW, HALF)
        and kernel.shape == (3, 3, 3, IN, OUT)
    )


def on_device(latent, norm_gain, norm_shift, kernel, conv_bias, blend_profile):
    arguments = (latent, norm_gain, norm_shift, kernel, conv_bias, blend_profile)
    if fits_fused(latent, kernel):
        return fused_on_device(*arguments)
    return gathered_on_device(*arguments)


def solution(mesh):
    in_specs = (
        P(("grp", "tm"), None, "tile", "ch"),
        P("ch"),
        P("ch"),
        P(None, None, None, ("ch", "tile", "tm"), None),
        P("ch"),
        P(),
    )
    out_specs = P(("grp", "tm"), None, "tile", "ch")
    return jax.shard_map(
        on_device, mesh=mesh, in_specs=in_specs, out_specs=out_specs, check_vma=False
    )
```

```python
import functools
import jax
import jax.numpy as jnp
from jax import lax
from jax.experimental import pallas as pl
from jax.experimental.pallas import tpu as pltpu
from jax.sharding import PartitionSpec as P

GROUPS = 32
RIM = 4


def with_halo(shard, sides, width):
    for axis, dim in sides:
        size, length = (lax.axis_size(axis), shard.shape[dim])
        up = [(i, (i + 1) % size) for i in range(size - 1)]
        down = [(j, i) for i, j in up]
        last = lax.slice_in_dim(shard, length - width, length, axis=dim)
        leading = lax.slice_in_dim(shard, 0, width, axis=dim)
        before = lax.ppermute(last, axis, up)
        after = lax.ppermute(leading, axis, down)
        shard = jnp.concatenate([before, shard, after], axis=dim)
    return shard


def passed_along(block, axis, distance):
    devices = range(lax.axis_size(axis))
    route = [(i - distance, i) for i in devices if i - distance in devices]
    return lax.ppermute(block, axis, route)


def ramp_weight(profile, position, margin):
    fraction = (position.astype(jnp.float32) + 0.5) / (2.0 * margin)
    exponent = 1.0 + profile.astype(jnp.float32)
    near_part = jnp.power(1.0 - fraction, exponent)
    far_part = jnp.power(fraction, exponent)
    return near_part / (near_part + far_part)


def frame_stats(values, colmask, groups):
    frame_count, row_count, col_count, chan_count = values.shape
    grouped = values.reshape(frame_count, row_count, col_count, groups, chan_count // groups)
    weight = colmask.reshape(1, 1, col_count, 1, 1)
    counted = row_count * (chan_count // groups) * jnp.sum(colmask)
    center = jnp.sum(grouped * weight, axis=(1, 2, 4)) / counted
    spread = (grouped - center[:, None, None, :, None]) * weight
    inverse = lax.rsqrt(jnp.sum(spread * spread, axis=(1, 2, 4)) / counted + 1e-06)
    return (center, inverse)


def activate(values, center, inverse, norm_gain, norm_shift, colmask, timemask, groups):
    frame_count, row_count, col_count, chan_count = values.shape
    grouped = values.reshape(frame_count, row_count, col_count, groups, chan_count // groups)
    normed = (grouped - center[:, None, None, :, None]) * inverse[:, None, None, :, None]
    normed = normed.reshape(values.shape) * norm_gain + norm_shift
    masked = jax.nn.silu(normed) * colmask[None, None, :, None] * timemask[:, None, None, None]
    return masked.astype(jnp.bfloat16)


def conv_taps(padded, kernel_part, frame_count, row_count, col_count):
    in_width = kernel_part.shape[3]
    running = None
    for tap_time in range(3):
        for tap_row in range(3):
            for tap_col in range(3):
                window = padded[
                    tap_time : tap_time + frame_count,
                    tap_row : tap_row + row_count,
                    tap_col : tap_col + col_count,
                ]
                contrib = jnp.dot(
                    window.reshape(-1, in_width),
                    kernel_part[tap_time, tap_row, tap_col],
                    preferred_element_type=jnp.float32,
                )
                running = contrib if running is None else running + contrib
    return running


def gathered_on_device(latent, norm_gain, norm_shift, kernel, conv_bias, blend_profile):
    frame_count, row_count, core_cols, chan_half = latent.shape
    out_chans = kernel.shape[4]
    groups = GROUPS // lax.axis_size("ch")
    ncols = core_cols + 2 * RIM
    tile_pos = lax.axis_index("tile")
    tile_count = lax.axis_size("tile")
    window_in = with_halo(latent, (("tile", 2),), RIM)
    cached = passed_along(window_in, "tm", 1)
    frames = jnp.concatenate([cached, window_in], axis=0).astype(jnp.float32)
    column = tile_pos * core_cols - RIM + jnp.arange(ncols, dtype=jnp.int32)
    colmask = ((column >= 0) & (column < tile_count * core_cols)).astype(jnp.float32)
    started = (lax.axis_index("tm") > 0).astype(jnp.float32)
    timemask = jnp.concatenate(
        [jnp.ones((2,), jnp.float32) * started, jnp.ones((frame_count,), jnp.float32)]
    )
    center, inverse = frame_stats(frames, colmask, groups)
    activated = activate(frames, center, inverse, norm_gain, norm_shift, colmask, timemask, groups)
    inputs = (jnp.pad(activated, ((0, 0), (1, 1), (1, 1), (0, 0))),)
    widths = (ncols,)

    def accumulate(shard_rows):
        return tuple(
            (
                conv_taps(source, shard_rows, frame_count, row_count, width_cols)
                for source, width_cols in zip(inputs, widths)
            )
        )

    totals = accumulate(lax.all_gather(kernel, ("tile", "tm"), axis=3, tiled=True))
    shaped = [
        running.reshape(frame_count, row_count, width_cols, out_chans)
        for running, width_cols in zip(totals, widths)
    ]
    joined = shaped[0]
    summed = lax.psum_scatter(joined, "ch", scatter_dimension=3, tiled=True)
    tile_out = (summed + conv_bias).astype(jnp.bfloat16)
    extended = with_halo(tile_out, (("tile", 2),), RIM)
    own_out = tile_out[:, :, RIM : RIM + core_cols]
    left_nbr = extended[:, :, :RIM]
    right_nbr = extended[:, :, ncols + RIM :]
    own_profile = lax.dynamic_index_in_dim(blend_profile, tile_pos, 0, keepdims=False)
    prev_profile = lax.dynamic_index_in_dim(
        blend_profile, jnp.maximum(tile_pos - 1, 0), 0, keepdims=False
    )
    offsets = jnp.arange(RIM, dtype=jnp.int32)
    left_weight = jnp.where(tile_pos > 0, ramp_weight(prev_profile, offsets + RIM, RIM), 0.0)
    right_weight = jnp.where(tile_pos < tile_count - 1, ramp_weight(own_profile, offsets, RIM), 1.0)
    left_wide = left_weight[None, None, :, None]
    right_wide = right_weight[None, None, :, None]
    own_float = own_out.astype(jnp.float32)
    head_cols = own_float[:, :, :RIM] * (1.0 - left_wide) + left_nbr.astype(jnp.float32) * left_wide
    tail_cols = own_float[:, :, core_cols - RIM :] * right_wide + right_nbr.astype(jnp.float32) * (
        1.0 - right_wide
    )
    middle = own_float[:, :, RIM : core_cols - RIM]
    return jnp.concatenate([head_cols, middle, tail_cols], axis=2).astype(jnp.bfloat16)


MESH = pl.DeviceIdType.MESH
TILES = 4
BLOCKS = 2
PARTS = TILES * BLOCKS
ROWS = 8
TW = 16
WIN = TW + 2 * RIM
IN = 32
FRAMES = 4
HALF = 256
OUT = 512
F32 = jnp.float32
BF16 = jnp.bfloat16


def iota(shape, dim):
    return lax.broadcasted_iota(jnp.int32, shape, dim)


def exact_dot(a, b):
    return jnp.dot(a, b, preferred_element_type=F32, precision=lax.Precision.HIGHEST)


def fused_kernel(
    profile_in, latent_in, gain_in, shift_in, kernel, bias_in, out,
    profile, latent, gain, shift, bias,
    weights, packed, arrived, grid, act, sums, centers, inverses, ramp, lhs, conv,
    keep, give, took, cross, crossed, send, landed,
    i_sem, w_sem, a_send, a_recv, s_send, s_recv, x_send, x_recv, z_send, z_recv,
):
    tile = lax.axis_index("tile")
    tm = lax.axis_index("tm")
    ch = lax.axis_index("ch")
    me = tile * BLOCKS + tm

    inputs = [
        pltpu.make_async_copy(source, target, i_sem.at[n])
        for n, (source, target) in enumerate(
            (
                (latent_in, latent), (profile_in, profile), (gain_in, gain),
                (shift_in, shift), (bias_in, bias),
            )
        )
    ]
    for load in inputs:
        load.start()
    loads = []
    for a in range(3):
        for e in range(3):
            for side in range(2):
                start = pl.multiple_of(((ch + side) % 2) * HALF, HALF)
                loads.append(
                    pltpu.make_async_copy(
                        kernel.at[a, :, e, :, pl.ds(start, HALF)],
                        weights.at[a * 3 + e, pl.ds(0, 3), :, pl.ds(side * HALF, HALF)],
                        w_sem.at[(a * 3 + e) * 2 + side],
                    )
                )
    for load in loads:
        load.start()

    barrier = pltpu.get_barrier_semaphore()
    for d in range(1, PARTS):
        j = (me + d) % PARTS
        pl.semaphore_signal(
            barrier, inc=1, device_id={"tile": j // BLOCKS, "tm": j % BLOCKS}, device_id_type=MESH
        )
    pl.semaphore_signal(barrier, inc=1, device_id={"ch": 1 - ch}, device_id_type=MESH)

    row_i, col_i = iota((128, 128), 0), iota((128, 128), 1)
    turn = jnp.where((row_i % ROWS) * TW + row_i // ROWS == col_i, 1.0, 0.0).astype(BF16)
    lane_block = iota((64, 128), 1) // IN
    inputs[0].wait()
    turned = [
        jnp.dot(turn, latent[f].reshape(ROWS * TW, HALF), preferred_element_type=F32)
        for f in range(2)
    ]
    for j in range(PARTS):
        lanes = slice((j // 4) * 128, (j // 4) * 128 + 128)
        joined = None
        for k in range(4):
            piece = turned[k // 2][(k % 2) * 64 : (k % 2) * 64 + 64, lanes]
            amount = ((k - j % 4) * IN) % 128
            if amount:
                piece = pltpu.roll(piece, amount, 1)
            joined = piece if joined is None else jnp.where(lane_block == k, piece, joined)
        packed[j] = joined.astype(BF16)

    pl.semaphore_wait(barrier, PARTS)
    moves = []
    for d in range(1, PARTS):
        j = (me + d) % PARTS
        moves.append(
            pltpu.make_async_remote_copy(
                src_ref=packed.at[j],
                dst_ref=arrived.at[me],
                send_sem=a_send.at[d - 1],
                recv_sem=a_recv.at[d - 1],
                device_id={"tile": j // BLOCKS, "tm": j % BLOCKS},
                device_id_type=MESH,
            )
        )
    for move in moves:
        move.start()
    arrived[me] = packed[me]

    act[:, 0:2] = jnp.zeros((TILES, 2, WIN + 2, ROWS, 128), F32)
    act[:, 2:, 0:1] = jnp.zeros((TILES, FRAMES, 1, ROWS, 128), F32)
    act[:, 2:, WIN + 1 :] = jnp.zeros((TILES, FRAMES, 1, ROWS, 128), F32)
    grid[:, 0:RIM] = jnp.zeros((FRAMES, RIM, ROWS, 128), F32)
    grid[:, RIM + TILES * TW :] = jnp.zeros((FRAMES, RIM, ROWS, 128), F32)
    weights[:, 3] = jnp.zeros((9, IN, OUT), BF16)
    for load in inputs[1:]:
        load.wait()
    fraction = (iota((8, OUT), 0).astype(F32) + 0.5) / (2.0 * RIM)
    for margin in range(TILES):
        p = jnp.full((8, OUT), profile[margin], jnp.int32)
        near, far = 1.0 - fraction, fraction
        near_part, far_part = near, far
        for power in range(1, 4):
            near_part = jnp.where(p >= power, near_part * near, near_part)
            far_part = jnp.where(p >= power, far_part * far, far_part)
        ramp[margin] = near_part / (near_part + far_part)
    pick = jnp.where(iota((HALF, 128), 0) == me * IN + iota((HALF, 128), 1) % IN, 1.0, 0.0)
    own_gain = exact_dot(jnp.broadcast_to(gain[...], (8, HALF)), pick)
    own_shift = exact_dot(jnp.broadcast_to(shift[...], (8, HALF)), pick)
    group = jnp.where(
        (row_i // (IN // 2)) == (col_i // (IN // 2)), 1.0, 0.0
    )
    spread = [
        jnp.where((row_i // IN == k) & (row_i % IN == col_i % IN), 1.0, 0.0).astype(BF16)
        for k in range(4)
    ]

    for move in moves:
        move.wait()
    everything = arrived[...].reshape(PARTS * 64, 128)
    for k in range(4):
        wide = jnp.dot(everything, spread[k], preferred_element_type=F32)
        for s in range(PARTS):
            first = RIM + (s // BLOCKS) * TW + (k % 2) * (TW // 2)
            grid[(s % BLOCKS) * 2 + k // 2, first : first + TW // 2] = wide[
                s * 64 : s * 64 + 64
            ].reshape(TW // 2, ROWS, 128)

    def present(t):
        column = t * TW + iota((WIN, ROWS, 128), 0)
        return jnp.where((column >= RIM) & (column < RIM + TILES * TW), 1.0, 0.0)

    def totals(n, _):
        t, f = n // FRAMES, n % FRAMES
        sums[n] = jnp.sum(grid[f, pl.ds(t * TW, WIN)], axis=0)
        return 0

    pairs = TILES * FRAMES
    tile_of = iota((pairs, 1, 128), 0) // FRAMES
    counted = jnp.where((tile_of == 0) | (tile_of == TILES - 1), WIN - RIM, WIN).astype(F32)
    counted = counted * float(ROWS * (IN // 2))
    lax.fori_loop(0, pairs, totals, 0)

    def grouped():
        per_group = exact_dot(sums[...].reshape(pairs * ROWS, 128), group)
        return jnp.sum(per_group.reshape(pairs, ROWS, 128), axis=1, keepdims=True) / counted

    centers[...] = jnp.broadcast_to(grouped(), (pairs, ROWS, 128))

    def squares(n, _):
        t, f = n // FRAMES, n % FRAMES
        apart = (grid[f, pl.ds(t * TW, WIN)] - centers[n]) * present(t)
        sums[n] = jnp.sum(apart * apart, axis=0)
        return 0

    lax.fori_loop(0, pairs, squares, 0)
    inverses[...] = jnp.broadcast_to(lax.rsqrt(grouped() + 1e-06), (pairs, ROWS, 128))

    block_of, row_of = iota((ROWS, 128), 1) // IN, iota((ROWS, 128), 0)
    inside = (block_of == 1) | ((block_of == 0) & (row_of > 0))
    inside = jnp.where(inside | ((block_of == 2) & (row_of < ROWS - 1)), 1.0, 0.0)

    def activate_window(n, _):
        t, f = n // FRAMES, n % FRAMES
        v = (grid[f, pl.ds(t * TW, WIN)] - centers[n]) * inverses[n] * own_gain + own_shift
        v = v / (1.0 + jnp.exp(-v)) * present(t)
        before, after = pltpu.roll(v, 1, 1), pltpu.roll(v, ROWS - 1, 1)
        v = jnp.where(block_of == 0, before, jnp.where(block_of == 2, after, v))
        act[t, f + 2, 1 : WIN + 1] = v * inside
        return 0

    lax.fori_loop(0, pairs, activate_window, 0)
    for load in loads:
        load.wait()

    def target(i):
        upper = 1 - i // 2
        lower = ((i + 1) // 2) % 2
        return 2 * ((tile // 2 + upper) % 2) + (tile % 2 + lower) % 2

    def next_stop(i):
        later = (i + 1) // 2
        later = later - later // 2
        return later * target(i) + (1 - later) * (2 * tile + 1 - 5 * (tile // 2))

    inner = (tile == 1) | (tile == 2)

    def sibling_copy(i, part):
        return pltpu.make_async_remote_copy(
            src_ref=give.at[i, part], dst_ref=took.at[i, part],
            send_sem=s_send.at[i * 2 + part], recv_sem=s_recv.at[i * 2 + part],
            device_id={"ch": 1 - ch}, device_id_type=MESH,
        )

    def cross_copy(i):
        return pltpu.make_async_remote_copy(
            src_ref=cross.at[i], dst_ref=crossed.at[i],
            send_sem=x_send.at[i], recv_sem=x_recv.at[i],
            device_id={"tm": 1 - tm}, device_id_type=MESH,
        )

    def owner_copy(i):
        return pltpu.make_async_remote_copy(
            src_ref=send.at[i], dst_ref=landed.at[i],
            send_sem=z_send.at[i], recv_sem=z_recv.at[i],
            device_id={"tile": next_stop(i)}, device_id_type=MESH,
        )

    def convolve(i, part):
        start = ((tm + 1 + part) % BLOCKS) * 2
        t = target(i)
        left, right = (t + TILES - 1) % TILES, (t + 1) % TILES
        for f in range(2):
            for a in range(3):
                for e in range(3):
                    lanes = slice((a * 3 + e) * 128, (a * 3 + e) * 128 + 128)
                    row = f * WIN * ROWS
                    for owner, first, count in (
                        (t, RIM, TW), (left, TW + RIM, RIM), (right, 0, RIM),
                    ):
                        piece = act[owner, start + f + a, first + e : first + e + count]
                        lhs[row : row + count * ROWS, lanes] = piece.reshape(
                            count * ROWS, 128
                        ).astype(BF16)
                        row += count * ROWS
        conv[...] = jnp.dot(
            lhs[...], weights[...].reshape(9 * 128, OUT), preferred_element_type=F32
        )
        has_left = jnp.where(t > 0, 1.0, 0.0)
        has_right = jnp.where(t < TILES - 1, 1.0, 0.0)
        for f in range(2):
            base = f * WIN * ROWS
            for c in range(TW):
                value = conv[base + c * ROWS : base + (c + 1) * ROWS]
                if c < RIM:
                    w = ramp[left, RIM + c : RIM + c + 1] * has_left
                    far = base + (TW + c) * ROWS
                    value = value * (1.0 - w) + conv[far : far + ROWS] * w
                if c >= TW - RIM:
                    j = c - (TW - RIM)
                    w = 1.0 - (1.0 - ramp[t, j : j + 1]) * has_right
                    far = base + (TW + RIM + j) * ROWS
                    value = value * w + conv[far : far + ROWS] * (1.0 - w)
                row = (f * TW + c) * ROWS
                keep[i, part, row : row + ROWS] = value[:, :HALF]
                give[i, part, row : row + ROWS] = value[:, HALF:].astype(BF16)
        sibling_copy(i, part).start()

    def join_sibling(i):
        sibling_copy(i, 0).wait_recv()
        cross[i] = (keep[i, 0] + took[i, 0].astype(F32)).astype(BF16)
        cross_copy(i).start()

    def join_cross(i):
        sibling_copy(i, 1).wait_recv()
        cross_copy(i).wait_recv()
        return keep[i, 1] + took[i, 1].astype(F32) + crossed[i].astype(F32)

    def pass_on(i):
        value = join_cross(i)
        send[i] = value.astype(BF16)

        @pl.when((i == 1) & inner)
        def _():
            owner_copy(0).wait_recv()
            send[i] = (value + landed[0].astype(F32)).astype(BF16)

        owner_copy(i).start()

    def step(s, _):
        convolve(s, 0)
        convolve(s, 1)
        join_sibling(s)
        pl.when(s >= 1)(lambda: pass_on(s - 1))
        return 0

    lax.fori_loop(0, TILES, step, 0)
    total = join_cross(TILES - 1)

    @pl.when(jnp.logical_not(inner))
    def _():
        owner_copy(0).wait_recv()

    total = total + jnp.where(inner, 0.0, landed[0].astype(F32))
    for i in range(1, TILES - 1):
        owner_copy(i).wait_recv()
        total = total + landed[i].astype(F32)
    result = (total + bias[...]).astype(BF16)
    back = jnp.where((row_i % TW) * ROWS + row_i // TW == col_i, 1.0, 0.0).astype(BF16)
    for f in range(2):
        frame = result[f * TW * ROWS : (f + 1) * TW * ROWS]
        out[f] = (
            jnp.dot(back, frame, preferred_element_type=F32)
            .astype(BF16)
            .reshape(ROWS, TW, HALF)
        )
    for i in range(TILES):
        sibling_copy(i, 0).wait_send()
        sibling_copy(i, 1).wait_send()
        cross_copy(i).wait_send()
        if i < TILES - 1:
            owner_copy(i).wait_send()


def fused_on_device(latent, norm_gain, norm_shift, kernel, conv_bias, blend_profile):
    block_rows = 2 * TW * ROWS
    dma = pltpu.SemaphoreType.DMA
    hbm = pl.BlockSpec(memory_space=pltpu.MemorySpace.HBM)
    vector = pltpu.VMEM((1, HALF), F32)
    return pl.pallas_call(
        fused_kernel,
        out_shape=jax.ShapeDtypeStruct((2, ROWS, TW, HALF), BF16),
        in_specs=[hbm] * 6,
        out_specs=pl.BlockSpec(memory_space=pltpu.VMEM),
        scratch_shapes=[
            pltpu.SMEM((TILES,), jnp.int32),
            pltpu.VMEM((2, ROWS, TW, HALF), BF16),
            vector, vector, vector,
            pltpu.VMEM((9, 4, IN, OUT), BF16),
            pltpu.VMEM((PARTS, 64, 128), BF16),
            pltpu.VMEM((PARTS, 64, 128), BF16),
            pltpu.VMEM((FRAMES, TILES * TW + 2 * RIM, ROWS, 128), F32),
            pltpu.VMEM((TILES, FRAMES + 2, WIN + 2, ROWS, 128), F32),
            pltpu.VMEM((TILES * FRAMES, ROWS, 128), F32),
            pltpu.VMEM((TILES * FRAMES, ROWS, 128), F32),
            pltpu.VMEM((TILES * FRAMES, ROWS, 128), F32),
            pltpu.VMEM((TILES, 2 * RIM, OUT), F32),
            pltpu.VMEM((2 * WIN * ROWS, 9 * 128), BF16),
            pltpu.VMEM((2 * WIN * ROWS, OUT), F32),
            pltpu.VMEM((TILES, 2, block_rows, HALF), F32),
            pltpu.VMEM((TILES, 2, block_rows, HALF), BF16),
            pltpu.VMEM((TILES, 2, block_rows, HALF), BF16),
            pltpu.VMEM((TILES, block_rows, HALF), BF16),
            pltpu.VMEM((TILES, block_rows, HALF), BF16),
            pltpu.VMEM((TILES - 1, block_rows, HALF), BF16),
            pltpu.VMEM((TILES - 1, block_rows, HALF), BF16),
            dma((5,)), dma((18,)), dma((PARTS - 1,)), dma((PARTS - 1,)),
            dma((2 * TILES,)), dma((2 * TILES,)), dma((TILES,)), dma((TILES,)),
            dma((TILES - 1,)), dma((TILES - 1,)),
        ],
        compiler_params=pltpu.CompilerParams(
            collective_id=0, has_side_effects=True, vmem_limit_bytes=63 * 2**20
        ),
    )(
        blend_profile, latent, norm_gain.reshape(1, HALF), norm_shift.reshape(1, HALF),
        kernel, conv_bias.reshape(1, HALF),
    )


def fits_fused(latent, kernel):
    sizes = tuple(lax.axis_size(axis) for axis in ("tile", "tm", "ch"))
    return (
        sizes == (TILES, BLOCKS, 2)
        and latent.shape == (2, ROWS, TW, HALF)
        and kernel.shape == (3, 3, 3, IN, OUT)
    )


def on_device(latent, norm_gain, norm_shift, kernel, conv_bias, blend_profile):
    arguments = (latent, norm_gain, norm_shift, kernel, conv_bias, blend_profile)
    if fits_fused(latent, kernel):
        return fused_on_device(*arguments)
    return gathered_on_device(*arguments)


def solution(mesh):
    in_specs = (
        P(("grp", "tm"), None, "tile", "ch"),
        P("ch"),
        P("ch"),
        P(None, None, None, ("ch", "tile", "tm"), None),
        P("ch"),
        P(),
    )
    out_specs = P(("grp", "tm"), None, "tile", "ch")
    return jax.shard_map(
        on_device, mesh=mesh, in_specs=in_specs, out_specs=out_specs, check_vma=False
    )
```
